128 devices in a mesh: dom: 128 (over y, x, z, core).
Axes of the slice: x: 4, y: 4, z: 4, core: 2. Of those that a mesh axis runs over, the one named last changes fastest.
Arguments:
- velocity: bfloat16 [3, 512, 65536], P(None, None, 'dom'), may hold values from -1.1953125 to 1.1953125
- inverse_sizes: float32 [3, 65536], P(None, 'dom'), may hold values from 0.5 to 2
- resample_x: float32 [2, 8, 8, 65536], P(None, None, None, 'dom'), may hold values from 0 to 0.25
- resample_y: float32 [2, 4, 8, 65536], P(None, None, None, 'dom'), may hold values from 0 to 0.25
- resample_z: float32 [2, 4, 8, 65536], P(None, None, None, 'dom'), may hold values from 0 to 0.25
- piece_target: int32 [2, 65536], P(None, 'dom'), may hold values from 0 to 511, as said below
- target_brick: int32 [65536, 1], P('dom'), may hold values from 0 to 127; in each aligned block of 512 rows (0 to 511, 512 to 1023, ...) at most 16 rows name the same one
- target_block: int32 [65536], P('dom'), may hold values from 0 to 2047
- brick_home: int32 [128], replicated, may hold values from 0 to 127, each once
Outputs:
- bricks: float32 [128, 2048, 128], P('dom')
The draws below stay inside these ranges and needn't reach their ends.
Inputs may be any that keep to these rules, and one draw needn't show every extreme that they name: `piece_target`: among the 2 x 512 entries of one device's columns every value appears exactly twice. `target_brick`: in the rows of one device no brick is named more than 16 times, and in some device's rows some brick is named exactly 16 times. `brick_home`: every device is the home of exactly one brick.
All inputs are finite; a program needn't handle non-finite values.
Results may differ from the reference program's by a relative error of at most 0.0023.
Values sent between devices are 32-bit elements; how exact they have to be, the bound alone decides.
A program may use at most 192 MiB of HBM per device.

```python
import math
import jax
import jax.numpy as jnp
import numpy as np
from jax import lax

LAYERS = 4
EYN = 8
EZN = 16
CROSS = 128
E_DEV = 512
ELEMS = 65536
NBRICKS = 128
BLOCKS = 2048
CAPT = 16


def draw_piece_target(key, part):
    per_dev = LAYERS * EYN * EZN
    devices = ELEMS // per_dev
    subkeys = jax.random.split(key, devices)

    def shuffled(single):
        return jax.random.permutation(single, 2 * per_dev)
    orders = jax.vmap(shuffled)(subkeys)
    targets = (orders // 2).astype(jnp.int32).reshape(devices, per_dev, 2)
    return jnp.transpose(targets, (2, 0, 1)).reshape(2, ELEMS)


def with_ends(values, key, low, top_value):
    longest = values.shape.index(max(values.shape))
    spots = []
    for shift in (0, 1):
        where = [jax.random.randint(jax.random.fold_in(key, axis), (), 0, length) for axis, length in enumerate(values.shape)]
        where[longest] = (where[longest] + shift) % values.shape[longest]
        spots.append(tuple(where))
    return values.at[spots[0]].set(low).at[spots[1]].set(top_value)


def block_levels(stream_key, dims, cuts, low, high):
    factor_of = 1.0
    for axis_at, blocks in cuts:
        draws = jax.random.uniform(jax.random.fold_in(jax.random.fold_in(stream_key, 6), axis_at), (blocks,), jnp.float32, low / len(cuts), high / len(cuts))
        factor_of = factor_of * jnp.repeat(jnp.exp(draws), dims[axis_at] // blocks).reshape((-1,) + (1,) * (len(dims) - 1 - axis_at))
    return factor_of


def routed_block(rng, own, number, rows, number_of, top, most, slope):
    order = jax.random.permutation(rng, number_of)
    heavy_load, usual = portions_of(number_of, rows * top, most, slope, True), portions_of(number_of, rows * top, most, slope, False)
    places = jnp.arange(number_of)

    def named(lengths, offset_by):
        used = int((lengths > 0).sum())
        fixed = max(1, used // 4)
        moved = fixed + (places - fixed + offset_by * (used - fixed)) % max(1, number_of - fixed)
        return jnp.zeros((number_of,), jnp.int32).at[order[jnp.where(places < fixed, places, moved)]].set(jnp.asarray(lengths, jnp.int32))

    lengths = jnp.where(number % 4 == 0, named(heavy_load, number // 4), named(usual, number - number // 4 - 1))
    mixed = jax.random.permutation(jax.random.fold_in(own, 3), number_of)
    source_of, taker = mixed[0:number_of // 2 * 2:2], mixed[1:number_of // 2 * 2:2]
    margin = jnp.minimum(lengths[source_of] - 1, most - lengths[taker]) // 2
    margin = jnp.where((source_of == order[0]) | (taker == order[0]) | (lengths[taker] == 0), 0, jnp.maximum(margin, 0))
    moved = jax.random.randint(jax.random.fold_in(own, 4), (number_of // 2,), 0, 1 << 20) % (margin + 1)
    lengths = lengths.at[source_of].add(-moved).at[taker].add(moved)
    members = jnp.searchsorted(jnp.cumsum(lengths), jnp.arange(rows * top), side="right").astype(jnp.int32)
    grid = members.reshape(top, rows).T
    grid = grid[jax.random.permutation(jax.random.fold_in(own, 1), rows)]
    offset_by = jax.random.randint(jax.random.fold_in(own, 2), (rows, 1), 0, top)
    return jnp.take_along_axis(grid, (jnp.arange(top)[None, :] + offset_by) % top, axis=1)


def portions_of(number_of, total, limit, skew, full):
    weights = [(1 << 20) // math.isqrt(standing ** skew) + 1 for standing in range(1, number_of + 1)]
    largest = limit if full else min(limit, max(-(-total // number_of), total * weights[0] // sum(weights)))
    least = 1 if total - largest >= number_of - 1 else 0
    holding, spare = [largest] + [least] * (number_of - 1), total - largest - least * (number_of - 1)
    while spare > 0:
        candidates = [i for i in range(1, number_of) if holding[i] < largest] or [i for i in range(1, number_of) if holding[i] < limit]
        mass, remaining = sum([weights[i] for i in candidates]), spare
        for i in candidates:
            addition = min(limit - holding[i], max(1, remaining * weights[i] // mass), spare)
            holding[i] = holding[i] + addition
            spare = spare - addition
    return np.array(holding)


def centred(rng, extent, deviation, limit, cuts=(), kind=jnp.bfloat16):
    drawn = deviation * jax.random.normal(rng, extent, jnp.float32)
    if cuts:
        drawn = drawn * block_levels(rng, extent, cuts, -0.22, 0.18)
    return jnp.clip(drawn, -limit, limit).astype(kind)


def setup_inputs(seed: int = 0) -> dict:
    arg_keys = jax.random.split(jax.random.key(seed), 10)
    velocity = centred(arg_keys[0], (3, 512, ELEMS), 0.2, 1.1953125, ((2, 128),))
    inverse_sizes = jnp.clip(jnp.exp(math.log(2.0) - 1.3862944 * jax.random.uniform(arg_keys[1], (3, ELEMS), jnp.float32) ** block_levels(arg_keys[1], (3, ELEMS), ((1, 128),), -0.2, 0.2)), 0.5, 2.0)
    resample_x = jnp.clip(0.25 * jax.random.uniform(arg_keys[2], (2, 8, 8, ELEMS), jnp.float32) ** block_levels(arg_keys[2], (2, 8, 8, ELEMS), ((3, 128),), -0.2, 0.2), 0.0, 0.25)
    resample_y = jnp.clip(0.25 * jax.random.uniform(arg_keys[3], (2, 4, 8, ELEMS), jnp.float32) ** block_levels(arg_keys[3], (2, 4, 8, ELEMS), ((3, 128),), -0.2, 0.2), 0.0, 0.25)
    resample_z = jnp.clip(0.25 * jax.random.uniform(arg_keys[4], (2, 4, 8, ELEMS), jnp.float32) ** block_levels(arg_keys[4], (2, 4, 8, ELEMS), ((3, 128),), -0.2, 0.2), 0.0, 0.25)
    piece_target = draw_piece_target(jax.random.fold_in(arg_keys[9], 71), 0)
    target_brick_keys = jax.random.split(jax.random.fold_in(arg_keys[6], 1), ELEMS // E_DEV)
    target_brick_turns = jax.random.permutation(jax.random.fold_in(arg_keys[6], 3), ELEMS // E_DEV)
    target_brick = jax.vmap(lambda own, number: routed_block(jax.random.fold_in(arg_keys[6], 2), own, number, E_DEV, NBRICKS, 1, CAPT, 2))(target_brick_keys, target_brick_turns).reshape((ELEMS, 1))
    target_block = with_ends(jax.random.randint(arg_keys[7], (ELEMS,), 0, BLOCKS), jax.random.fold_in(arg_keys[7], 1), 0, BLOCKS - 1).astype(jnp.int32)
    brick_home = jax.random.permutation(arg_keys[8], NBRICKS).astype(jnp.int32)
    return dict(velocity=velocity, inverse_sizes=inverse_sizes, resample_x=resample_x, resample_y=resample_y, resample_z=resample_z, piece_target=piece_target, target_brick=target_brick, target_block=target_block, brick_home=brick_home)


GLL_NODES = [-1.0, -0.8717401485096066, -0.5917001814331423, -0.2092992179024789, 0.2092992179024789, 0.5917001814331423, 0.8717401485096066, 1.0]

def derivative_operator():
    barycentric = []
    for first in range(8):
        product_term = 1.0
        for other in range(8):
            if other != first:
                product_term = product_term * (GLL_NODES[first] - GLL_NODES[other])
        barycentric.append(1.0 / product_term)
    matrix_rows = []
    for first in range(8):
        row_values = []
        for second in range(8):
            if second == first:
                row_values.append(0.0)
            else:
                row_values.append(barycentric[second] / barycentric[first] / (GLL_NODES[first] - GLL_NODES[second]))
        row_values[first] = -sum(row_values)
        matrix_rows.append(row_values)
    diff_matrix = np.array(matrix_rows)
    identity = np.eye(8)
    return np.concatenate([np.kron(np.kron(diff_matrix, identity), identity), np.kron(np.kron(identity, diff_matrix), identity), np.kron(np.kron(identity, identity), diff_matrix)], axis=0)

def stitch_stream(gradient, from_prev, from_next):
    low_face = gradient[:, 0]
    high_face = gradient[:, 7]
    from_below = jnp.concatenate([from_prev[:, :, None, :], high_face[:, :, :-1, :]], axis=2)
    from_above = jnp.concatenate([low_face[:, :, 1:, :], from_next[:, :, None, :]], axis=2)
    return gradient.at[:, 0].set(low_face + from_below).at[:, 7].set(high_face + from_above)

def middle_eigen(gradient):
    strain = [[0.5 * (gradient[first][second] + gradient[second][first]) for second in range(3)] for first in range(3)]
    rotation = [[0.5 * (gradient[first][second] - gradient[second][first]) for second in range(3)] for first in range(3)]
    moment = [[sum((strain[first][inner] * strain[inner][second] + rotation[first][inner] * rotation[inner][second] for inner in range(3))) for second in range(3)] for first in range(3)]
    mean_diag = (moment[0][0] + moment[1][1] + moment[2][2]) / 3.0
    shift_x = moment[0][0] - mean_diag
    shift_y = moment[1][1] - mean_diag
    shift_z = moment[2][2] - mean_diag
    offdiag = moment[0][1] * moment[0][1] + moment[0][2] * moment[0][2] + moment[1][2] * moment[1][2]
    spread = (shift_x * shift_x + shift_y * shift_y + shift_z * shift_z + 2.0 * offdiag) / 6.0
    determinant = shift_x * (shift_y * shift_z - moment[1][2] * moment[1][2]) - moment[0][1] * (moment[0][1] * shift_z - moment[1][2] * moment[0][2]) + moment[0][2] * (moment[0][1] * moment[1][2] - shift_y * moment[0][2])
    halfdet = 0.5 * determinant
    discrim = jnp.maximum(spread * spread * spread - halfdet * halfdet, 0.0)
    angles = jnp.arctan2(jnp.sqrt(discrim), halfdet) / 3.0
    radius = 2.0 * jnp.sqrt(spread)
    largest = mean_diag + radius * jnp.cos(angles)
    smallest = mean_diag + radius * jnp.cos(angles + 2.0 * math.pi / 3.0)
    return 3.0 * mean_diag - largest - smallest

def resample(lambda_two, weight_x, weight_y, weight_z):
    highest = lax.Precision.HIGHEST
    along_x = jnp.einsum('oaie,ijke->oajke', weight_x, lambda_two, precision=highest)
    along_y = jnp.einsum('obje,oajke->oabke', weight_y, along_x, precision=highest)
    along_z = jnp.einsum('ocke,oabke->oabce', weight_z, along_y, precision=highest)
    columns = lambda_two.shape[-1]
    return jnp.transpose(along_z.reshape(2, 128, columns), (0, 2, 1))

def slab_gradients(operator, slab_velocity, slab_sizes):
    products = jnp.einsum('pq,cqe->cpe', operator.astype(jnp.float32), slab_velocity.astype(jnp.float32), precision=lax.Precision.HIGHEST)
    columns = slab_velocity.shape[2]
    scaled = products.reshape(3, 3, 512, columns) * slab_sizes[None, :, None, :]
    return scaled.reshape(9, 8, 64, LAYERS, CROSS)

def stitch_cross_grid(gradient):
    shaped = gradient.reshape(9, 8, 8, 8, LAYERS, EYN, EZN)
    low_face = shaped[:, :, 0]
    high_face = shaped[:, :, 7]
    zero_row = jnp.zeros_like(high_face[..., :1, :])
    from_below = jnp.concatenate([zero_row, high_face[..., :-1, :]], axis=-2)
    from_above = jnp.concatenate([low_face[..., 1:, :], zero_row], axis=-2)
    shaped = shaped.at[:, :, 0].set(low_face + from_below).at[:, :, 7].set(high_face + from_above)
    low_face = shaped[:, :, :, 0]
    high_face = shaped[:, :, :, 7]
    shaped = shaped.at[:, :, :, 0].set(low_face + jnp.roll(high_face, 1, axis=-1)).at[:, :, :, 7].set(high_face + jnp.roll(low_face, -1, axis=-1))
    points = jnp.arange(8, dtype=jnp.int32)
    on_face = (points == 0) | (points == 7)
    normal = jnp.arange(EYN, dtype=jnp.int32)
    at_wall = (points[:, None] == 0) & (normal[None, :] == 0) | (points[:, None] == 7) & (normal[None, :] == EYN - 1)
    mult_x = jnp.where(on_face, 2.0, 1.0)
    mult_y = jnp.where(on_face[:, None] & jnp.logical_not(at_wall), 2.0, 1.0)
    shaped = shaped / mult_x[None, :, None, None, None, None, None]
    shaped = shaped / mult_y[None, None, :, None, None, :, None]
    shaped = shaped / mult_x[None, None, None, :, None, None, None]
    return shaped

def reference(velocity, inverse_sizes, resample_x, resample_y, resample_z, piece_target, target_brick, target_block, brick_home):
    operator = jnp.asarray(derivative_operator(), jnp.float32).astype(jnp.bfloat16)
    per_dev = LAYERS * CROSS
    slabs = velocity.shape[2] // per_dev

    def by_slab(values):
        leading = values.shape[:-1]
        return jnp.moveaxis(values.reshape(leading + (slabs, per_dev)), -2, 0)
    vel_slabs = by_slab(velocity)
    size_slabs = by_slab(inverse_sizes)

    def rim_pass(inputs):
        gradient = slab_gradients(operator, inputs[0], inputs[1])
        return jnp.stack([gradient[:, 0, :, 0, :], gradient[:, 7, :, LAYERS - 1, :]], axis=2)
    rim_faces = lax.map(rim_pass, (vel_slabs, size_slabs))
    from_prev = jnp.roll(rim_faces[:, :, :, 1, :], 1, axis=0)
    from_next = jnp.roll(rim_faces[:, :, :, 0, :], -1, axis=0)

    def piece_pass(inputs):
        slab_vel, slab_size, weight_x, weight_y, weight_z, prev_face, next_face = inputs
        gradient = slab_gradients(operator, slab_vel, slab_size)
        gradient = stitch_stream(gradient, prev_face, next_face)
        gradient = stitch_cross_grid(gradient)
        lambda_two = middle_eigen(gradient.reshape(3, 3, 512, per_dev))
        return resample(lambda_two.reshape(8, 8, 8, per_dev), weight_x, weight_y, weight_z)
    pieces = lax.map(piece_pass, (vel_slabs, size_slabs, by_slab(resample_x), by_slab(resample_y), by_slab(resample_z), from_prev, from_next))
    local_ids = jnp.moveaxis(piece_target.reshape(2, slabs, per_dev), 1, 0)
    offsets = (jnp.arange(slabs, dtype=jnp.int32) * per_dev)[:, None, None]
    targets = (local_ids + offsets).reshape(-1).astype(jnp.int32)
    home_rows = brick_home[target_brick[targets, 0]]
    blocks = target_block[targets]
    bricks = jnp.zeros((NBRICKS, BLOCKS, 128), jnp.float32)
    return bricks.at[home_rows, blocks].add(pieces.reshape(-1, 128))
```

```python
import functools

import jax
import jax.numpy as jnp
import numpy as np
from jax import lax
from jax.experimental import pallas as pl
from jax.experimental.pallas import tpu as pltpu
from jax.sharding import PartitionSpec as P

EYN = 8
EZN = 16
BLOCKS = 2048
CROSS = 128
LAYERS = 4
SLOTS = 16
BF = jnp.bfloat16
F32 = jnp.float32
I32 = jnp.int32

GLL_NODES = [
    -1.0,
    -0.8717401485096066,
    -0.5917001814331423,
    -0.2092992179024789,
    0.2092992179024789,
    0.5917001814331423,
    0.8717401485096066,
    1.0,
]

SINE_POLY = (
    0.6666666865348816,
    -0.2716042101383209,
    0.18378925323486328,
    -0.1428457647562027,
    0.11690858751535416,
    -0.09370578080415726,
    0.06620869785547256,
    -0.03593844175338745,
    0.012577426619827747,
    -0.002056414494290948,
)


def diff_matrix():
    nodes = GLL_NODES
    weights = []
    for first in range(8):
        product_term = 1.0
        for other in range(8):
            if other != first:
                product_term = product_term * (nodes[first] - nodes[other])
        weights.append(1.0 / product_term)
    rows = []
    for first in range(8):
        row = []
        for second in range(8):
            if second == first:
                row.append(0.0)
            else:
                row.append(weights[second] / weights[first] / (nodes[first] - nodes[second]))
        row[first] = -sum(row)
        rows.append(row)
    return np.array(rows)


def iota(shape, dim):
    return lax.broadcasted_iota(I32, shape, dim)


def onehot(mask):
    return jnp.where(mask, 1.0, 0.0).astype(BF)


def dot(a, b):
    return jnp.dot(a, b, preferred_element_type=F32)


def dot_nt(a, b):
    return lax.dot_general(a, b, (((1,), (1,)), ((), ())), preferred_element_type=F32)


def prep_kernel(
    vel, opface, inv, target_of, brick_of, block_of, home_of,
    low, high, low_rim, high_rim, slots, block_rows,
):
    for layer in range(LAYERS):
        lanes = slice(CROSS * layer, CROSS * layer + CROSS)
        columns = jnp.concatenate([vel[c, :, lanes] for c in range(3)], axis=1)
        faces = dot(opface[...], columns)
        for c in range(3):
            for a in range(3):
                size = inv[a : a + 1, lanes]
                low_face = faces[64 * a : 64 * a + 64, CROSS * c : CROSS * c + CROSS] * size
                high_face = faces[192 + 64 * a : 256 + 64 * a, CROSS * c : CROSS * c + CROSS] * size
                if layer == 0:
                    low_rim[3 * c + a] = low_face
                else:
                    low[layer - 1, 3 * c + a] = low_face
                if layer == LAYERS - 1:
                    high_rim[3 * c + a] = high_face
                else:
                    high[layer, 3 * c + a] = high_face

    me = lax.axis_index("dom")
    brick_row = brick_of[...]
    same = iota((128, 512), 0) == brick_row
    member = onehot(same)
    earlier = onehot(iota((512, 512), 0) < iota((512, 512), 1))
    ordinal = jnp.sum(jnp.where(same, dot(member, earlier), 0.0), axis=0, keepdims=True)
    homes = jnp.broadcast_to(home_of[...].astype(F32), (8, 128)).astype(BF)
    home = dot(homes, member)[0:1]
    row = iota((8, 512), 0)
    pair = jnp.where(row == 0, home, jnp.where(row == 1, ordinal, 0.0)).astype(BF)
    for o in range(2):
        chosen = onehot(iota((512, 512), 0) == target_of[o : o + 1, :])
        picked = dot(pair, chosen)
        slots[o : o + 1, :] = (picked[0:1] * SLOTS + picked[1:2]).astype(I32)
    to_home = onehot(iota((128, 512), 0) == home.astype(I32))
    lane = ordinal.astype(I32) + SLOTS * lax.rem(me, 8)
    at_lane = iota((128, 512), 0) == lane
    block = block_of[...]
    upper = jnp.where(at_lane, (block // 16).astype(F32), 0.0).astype(BF)
    lower = jnp.where(at_lane, (block % 16).astype(F32), 0.0).astype(BF)
    block_rows[...] = dot_nt(to_home, upper) * 16.0 + dot_nt(to_home, lower)


def middle_eigen(j00, j01, j02, j10, j11, j12, j20, j21, j22):
    p01 = j01 * j10
    p02 = j02 * j20
    p12 = j12 * j21
    m00 = j00 * j00 + p01 + p02
    m11 = j11 * j11 + p01 + p12
    m22 = j22 * j22 + p02 + p12
    m01 = 0.5 * ((j00 + j11) * (j01 + j10) + j02 * j21 + j12 * j20)
    m02 = 0.5 * ((j00 + j22) * (j02 + j20) + j01 * j12 + j21 * j10)
    m12 = 0.5 * ((j11 + j22) * (j12 + j21) + j10 * j02 + j20 * j01)
    q = (m00 + m11 + m22) * (1.0 / 3.0)
    a00 = m00 - q
    a11 = m11 - q
    a22 = m22 - q
    s01 = m01 * m01
    s02 = m02 * m02
    s12 = m12 * m12
    s = (a00 * a00 + a11 * a11 + a22 * a22) * (1.0 / 6.0) + (s01 + s02 + s12) * (1.0 / 3.0)
    det = a00 * (a11 * a22 - s12) - a11 * s02 - a22 * s01 + 2.0 * (m01 * m02 * m12)
    h = 0.5 * det
    root = jnp.sqrt(s)
    disc = jnp.maximum(s * s * s - h * h, 0.0)
    z = h / jnp.maximum(s * root + jnp.sqrt(disc), 1e-37)
    w = z * z
    poly = SINE_POLY[-1]
    for coefficient in SINE_POLY[-2::-1]:
        poly = poly * w + coefficient
    return q - 2.0 * root * (z * poly)


def slab_layers(
    layers, vel, opx, opy, opz, inv, res_x, res_y, res_z, prevs, nexts, out_rows, out_lanes,
    grad, lam, stage_z, stage_y,
):
    columns = jnp.concatenate([v[c] for c in range(3) for v in vel], axis=1)
    count = len(layers)
    for a in range(3):
        for half in range(2):
            rows = slice(256 * half, 256 * half + 256)
            if a == 0:
                part = dot(opx[rows, :], columns)
            else:
                part = dot((opy if a == 1 else opz)[...], columns[rows, :])
            for c in range(3):
                for n, layer in enumerate(layers):
                    size = inv[a : a + 1, CROSS * layer : CROSS * layer + CROSS]
                    at = CROSS * (c * count + n)
                    grad[n, 3 * c + a, rows, :] = part[:, at : at + CROSS] * size
    for n in range(count):
        for m in range(9):
            grad[n, m, 0:64, :] = 0.5 * (grad[n, m, 0:64, :] + prevs[n][m])
            grad[n, m, 448:512, :] = 0.5 * (grad[n, m, 448:512, :] + nexts[n][m])

    lane = iota((8, CROSS), 1)
    normal = lane // EZN
    span = lane % EZN

    for n in range(count):

        def plane(i, carry, n=n):
            base = pl.multiple_of(i * 64, 64)
            for m in range(9):
                view = grad.at[n, m]
                first = view[pl.ds(base, 8), :]
                last = view[pl.ds(base + 56, 8), :]
                view[pl.ds(base, 8), :] = jnp.where(
                    normal > 0, 0.5 * (first + pltpu.roll(last, EZN, 1)), first
                )
                view[pl.ds(base + 56, 8), :] = jnp.where(
                    normal < EYN - 1, 0.5 * (last + pltpu.roll(first, CROSS - EZN, 1)), last
                )
                first = view[pl.ds(base, 8, stride=8), :]
                last = view[pl.ds(base + 7, 8, stride=8), :]
                before = jnp.where(
                    span == 0,
                    pltpu.roll(last, CROSS + 1 - EZN, 1),
                    pltpu.roll(last, 1, 1),
                )
                after = jnp.where(
                    span == EZN - 1,
                    pltpu.roll(first, EZN - 1, 1),
                    pltpu.roll(first, CROSS - 1, 1),
                )
                view[pl.ds(base, 8, stride=8), :] = 0.5 * (first + before)
                view[pl.ds(base + 7, 8, stride=8), :] = 0.5 * (last + after)
            for j in range(8):
                at = pl.ds(base + 8 * j, 8)
                lam[n, at, :] = middle_eigen(*[grad[n, m, at, :] for m in range(9)])
            return carry

        lax.fori_loop(0, 8, plane, 0)

    for n in range(count):
        for o in range(2):

            def along_z(i, carry, n=n, o=o):
                base = i * 64
                points = [lam[n, pl.ds(base + k, 8, stride=8), :] for k in range(8)]
                for w in range(4):
                    total = points[0] * res_z[n][o, w, 0:1, :]
                    for k in range(1, 8):
                        total = total + points[k] * res_z[n][o, w, k : k + 1, :]
                    stage_z[pl.ds(pl.multiple_of(w * 64 + i * 8, 8), 8), :] = total
                return carry

            lax.fori_loop(0, 8, along_z, 0)
            for w in range(4):
                points = [stage_z[pl.ds(w * 64 + j, 8, stride=8), :] for j in range(8)]
                for v in range(4):
                    total = points[0] * res_y[n][o, v, 0:1, :]
                    for j in range(1, 8):
                        total = total + points[j] * res_y[n][o, v, j : j + 1, :]
                    stage_y[32 * v + 8 * w : 32 * v + 8 * w + 8, :] = total
            points = [
                jnp.concatenate(
                    [stage_y[pl.ds(i, 8, stride=8), :], stage_y[pl.ds(64 + i, 8, stride=8), :]], axis=0
                )
                for i in range(8)
            ]
            for u in range(8):
                total = points[0] * res_x[n][o, u, 0:1, :]
                for i in range(1, 8):
                    total = total + points[i] * res_x[n][o, u, i : i + 1, :]
                upper = total.astype(BF)
                lower = (total - upper.astype(F32)).astype(BF)
                at = out_lanes(o, n)
                out_rows[16 * u : 16 * u + 16, at : at + CROSS] = upper
                out_rows[128 + 16 * u : 144 + 16 * u, at : at + CROSS] = lower


def inner_kernel(
    vel1, vel2, opx, opy, opz, inv, x1, x2, y1, y2, z1, z2, prevs, nexts,
    rows, grad, lam, stage_z, stage_y,
):
    slab_layers(
        (1, 2), (vel1, vel2), opx, opy, opz, inv, (x1, x2), (y1, y2), (z1, z2),
        (prevs.at[0], prevs.at[1]), (nexts.at[1], nexts.at[2]),
        rows, lambda o, n: 256 * o + 128 * n, grad, lam, stage_z, stage_y,
    )


def outer_kernel(
    vel0, vel3, opx, opy, opz, inv, x0, x3, y0, y3, z0, z3,
    prev0, prev3, next0, next3, inner_rows, slots, block_rows,
    send, rows, grad, lam, stage_z, stage_y,
):
    slab_layers(
        (0, 3), (vel0, vel3), opx, opy, opz, inv, (x0, x3), (y0, y3), (z0, z3),
        (prev0, prev3.at[0]), (next0.at[0], next3),
        rows, lambda o, n: 512 * o + 384 * n, grad, lam, stage_z, stage_y,
    )
    for o in range(2):
        rows[:, 512 * o + 128 : 512 * o + 384] = inner_rows[:, 256 * o : 256 * o + 256]
    slot_row = jnp.concatenate([slots[0:1, :], slots[1:2, :]], axis=1)

    def pack(g, carry):
        base = pl.multiple_of(g * 16, 16)
        chosen = onehot(iota((256, 1024), 0) + g * 256 == slot_row)
        packed = dot_nt(chosen, rows[...])
        send[pl.ds(base, 16), 0:SLOTS, :] = (packed[:, 0:128] + packed[:, 128:256]).reshape(16, SLOTS, 128)
        send[pl.ds(base, 16), SLOTS, :] = block_rows[pl.ds(base, 16), :]
        return carry

    lax.fori_loop(0, 8, pack, 0)


def exchange_kernel(source, landed, send_sem, recv_sem, own_sem):
    me = lax.axis_index("dom")
    count = lax.axis_size("dom")
    barrier = pltpu.get_barrier_semaphore()

    def greet(step, carry):
        pl.semaphore_signal(
            barrier, inc=1, device_id=(lax.rem(me + step, count),),
            device_id_type=pl.DeviceIdType.MESH,
        )
        return carry

    lax.fori_loop(1, count, greet, 0)
    own = pltpu.make_async_copy(source.at[me], landed.at[me], own_sem)
    own.start()
    pl.semaphore_wait(barrier, count - 1)

    def push(step, carry):
        peer = lax.rem(me + step, count)
        pltpu.make_async_remote_copy(
            src_ref=source.at[peer], dst_ref=landed.at[me], send_sem=send_sem, recv_sem=recv_sem,
            device_id=(peer,), device_id_type=pl.DeviceIdType.MESH,
        ).start()
        return carry

    lax.fori_loop(1, count, push, 0)
    own.wait()
    every = pltpu.make_async_remote_copy(
        src_ref=source.at[pl.ds(0, count - 1)], dst_ref=landed.at[pl.ds(0, count - 1)],
        send_sem=send_sem, recv_sem=recv_sem,
        device_id=(me,), device_id_type=pl.DeviceIdType.MESH,
    )
    every.wait_recv()
    every.wait_send()


def unpack_kernel(landed, bricks, rows, blocks):
    group = pl.program_id(0)

    @pl.when(group == 0)
    def _():
        blocks[...] = jnp.sum(landed[:, SLOTS, :].reshape(16, 8, 128), axis=1).astype(I32)
        for part in range(8):
            values = landed[16 * part : 16 * part + 16, 0:SLOTS, :].reshape(256, 128)
            upper = values.astype(BF)
            rows[256 * part : 256 * part + 256, 0:128] = upper
            rows[256 * part : 256 * part + 256, 128:256] = (values - upper.astype(F32)).astype(BF)

    place = iota((256, 256), 0) + group * 256
    total = None
    for part in range(8):
        named = jnp.concatenate(
            [blocks[2 * part : 2 * part + 1, :], blocks[2 * part + 1 : 2 * part + 2, :]], axis=1
        )
        term = dot(onehot(place == named), rows[256 * part : 256 * part + 256, :])
        total = term if total is None else total + term
    bricks[0] = total[:, 0:128] + total[:, 128:256]


def whole(shape, *indices):
    at = tuple(indices) if indices else (0,) * len(shape)
    return pl.BlockSpec(shape, lambda *_: at)


VLIMIT = pltpu.CompilerParams(vmem_limit_bytes=48 << 20)


def prepare(vel, inv, piece_target, target_brick, target_block, brick_home):
    d = diff_matrix()
    one = np.eye(8)
    opx = np.kron(np.kron(d, one), one)
    opy = np.kron(np.kron(one, d), one)
    opz = np.kron(np.kron(one, one), d)
    opface = np.concatenate([op[rows] for rows in (slice(0, 64), slice(448, 512)) for op in (opx, opy, opz)])
    opface = jnp.asarray(opface, F32).astype(BF)
    face = jax.ShapeDtypeStruct((9, 64, 128), F32)
    faces = jax.ShapeDtypeStruct((3, 9, 64, 128), F32)
    return pl.pallas_call(
        prep_kernel,
        out_shape=(faces, faces, face, face, jax.ShapeDtypeStruct((2, 512), I32),
                   jax.ShapeDtypeStruct((128, 128), F32)),
        compiler_params=VLIMIT,
        name="prep",
    )(vel, opface, inv, piece_target, target_brick.reshape(1, 512), target_block.reshape(1, 512),
      brick_home.reshape(1, 128))


def operators():
    d = diff_matrix()
    one = np.eye(8)
    opx = np.kron(np.kron(d, one), one)
    opy = np.kron(np.kron(np.eye(4), d), one)
    opz = np.kron(np.eye(32), d)
    return [jnp.asarray(op, F32).astype(BF) for op in (opx, opy, opz)]


def layer_specs(layers):
    specs = [whole((3, 512, 128), 0, 0, layer) for layer in layers]
    specs += [whole((512, 512)), whole((256, 256)), whole((256, 256)), whole((3, 512))]
    specs += [whole((2, 8, 8, 128), 0, 0, 0, layer) for layer in layers]
    specs += [whole((2, 4, 8, 128), 0, 0, 0, layer) for _ in range(2) for layer in layers]
    return specs


LAYER_SCRATCH = [
    pltpu.VMEM((2, 9, 512, 128), F32),
    pltpu.VMEM((2, 512, 128), F32),
    pltpu.VMEM((256, 128), F32),
    pltpu.VMEM((128, 128), F32),
]


def layer_args(vel, inv, res_x, res_y, res_z):
    return [vel, vel, *operators(), inv, res_x, res_x, res_y, res_y, res_z, res_z]


def inner(args, high, low):
    return pl.pallas_call(
        inner_kernel,
        grid=(1,),
        in_specs=layer_specs((1, 2)) + [whole((2, 9, 64, 128)), whole((3, 9, 64, 128))],
        out_specs=whole((256, 512)),
        out_shape=jax.ShapeDtypeStruct((256, 512), BF),
        scratch_shapes=LAYER_SCRATCH,
        compiler_params=VLIMIT,
        cost_estimate=pl.CostEstimate(flops=2_000_000_000, bytes_accessed=20_000_000, transcendentals=0),
        name="inner",
    )(*args, high, low)


def outer(args, from_prev, high, low, from_next, inner_rows, slots, block_rows):
    face = whole((9, 64, 128))
    return pl.pallas_call(
        outer_kernel,
        grid=(1,),
        in_specs=layer_specs((0, 3)) + [
            face, whole((1, 9, 64, 128), 2, 0, 0, 0), whole((1, 9, 64, 128)), face,
            whole((256, 512)), whole((2, 512)), whole((128, 128)),
        ],
        out_specs=whole((128, SLOTS + 1, 128)),
        out_shape=jax.ShapeDtypeStruct((128, SLOTS + 1, 128), F32),
        scratch_shapes=[pltpu.VMEM((256, 1024), BF)] + LAYER_SCRATCH,
        compiler_params=VLIMIT,
        cost_estimate=pl.CostEstimate(flops=4_000_000_000, bytes_accessed=20_000_000, transcendentals=0),
        name="outer",
    )(*args, from_prev, high, low, from_next, inner_rows, slots, block_rows)


def exchange(send):
    return pl.pallas_call(
        exchange_kernel,
        out_shape=jax.ShapeDtypeStruct(send.shape, send.dtype),
        in_specs=[pl.BlockSpec(memory_space=pl.ANY)],
        out_specs=pl.BlockSpec(memory_space=pl.ANY),
        scratch_shapes=[pltpu.SemaphoreType.DMA] * 3,
        compiler_params=pltpu.CompilerParams(collective_id=0, has_side_effects=True),
        name="exchange",
    )(send)


def unpack(landed):
    return pl.pallas_call(
        unpack_kernel,
        grid=(8,),
        in_specs=[whole((128, SLOTS + 1, 128))],
        out_specs=pl.BlockSpec((1, 256, 128), lambda g: (0, g, 0)),
        out_shape=jax.ShapeDtypeStruct((1, BLOCKS, 128), F32),
        scratch_shapes=[pltpu.VMEM((2048, 256), BF), pltpu.VMEM((16, 128), I32)],
        compiler_params=VLIMIT,
        name="unpack",
    )(landed)


def shards(
    velocity, inverse_sizes, resample_x, resample_y, resample_z,
    piece_target, target_brick, target_block, brick_home,
):
    count = lax.axis_size("dom")
    low, high, low_rim, high_rim, slots, block_rows = prepare(
        velocity, inverse_sizes, piece_target, target_brick, target_block, brick_home
    )
    from_prev = lax.ppermute(high_rim, "dom", [(i, (i + 1) % count) for i in range(count)])
    from_next = lax.ppermute(low_rim, "dom", [((i + 1) % count, i) for i in range(count)])
    args = layer_args(velocity, inverse_sizes, resample_x, resample_y, resample_z)
    inner_rows = inner(args, high, low)
    send = outer(args, from_prev, high, low, from_next, inner_rows, slots, block_rows)
    return unpack(exchange(send))


def solution(mesh):
    return jax.shard_map(
        shards,
        mesh=mesh,
        in_specs=(
            P(None, None, "dom"),
            P(None, "dom"),
            P(None, None, None, "dom"),
            P(None, None, None, "dom"),
            P(None, None, None, "dom"),
            P(None, "dom"),
            P("dom", None),
            P("dom"),
            P(),
        ),
        out_specs=P("dom", None, None),
        check_vma=False,
    )
```

```python
import jax
import jax.numpy as jnp
import numpy as np
from jax import lax
from jax.experimental import pallas as pl
from jax.experimental.pallas import tpu as pltpu
from jax.sharding import PartitionSpec as P

EYN = 8
EZN = 16
BLOCKS = 2048
CROSS = 128
LAYERS = 4
SLOTS = 16
BF = jnp.bfloat16
F32 = jnp.float32
I32 = jnp.int32

GLL_NODES = [
    -1.0,
    -0.8717401485096066,
    -0.5917001814331423,
    -0.2092992179024789,
    0.2092992179024789,
    0.5917001814331423,
    0.8717401485096066,
    1.0,
]

SINE_POLY = (
    0.6666666865348816,
    -0.2716042101383209,
    0.18378925323486328,
    -0.1428457647562027,
    0.11690858751535416,
    -0.09370578080415726,
    0.06620869785547256,
    -0.03593844175338745,
    0.012577426619827747,
    -0.002056414494290948,
)


def diff_matrix():
    nodes = GLL_NODES
    weights = []
    for first in range(8):
        product_term = 1.0
        for other in range(8):
            if other != first:
                product_term = product_term * (nodes[first] - nodes[other])
        weights.append(1.0 / product_term)
    rows = []
    for first in range(8):
        row = []
        for second in range(8):
            if second == first:
                row.append(0.0)
            else:
                row.append(weights[second] / weights[first] / (nodes[first] - nodes[second]))
        row[first] = -sum(row)
        rows.append(row)
    return np.array(rows)


def iota(shape, dim):
    return lax.broadcasted_iota(I32, shape, dim)


def onehot(mask):
    return jnp.where(mask, 1.0, 0.0).astype(BF)


def dot(a, b):
    return jnp.dot(a, b, preferred_element_type=F32)


def dot_nt(a, b):
    return lax.dot_general(a, b, (((1,), (1,)), ((), ())), preferred_element_type=F32)


def route(target_of, brick_of, block_of, home_of, slots, block_rows):
    me = lax.axis_index("dom")
    same = iota((128, 512), 0) == brick_of[...]
    member = onehot(same)
    earlier = onehot(iota((512, 512), 0) < iota((512, 512), 1))
    ordinal = jnp.sum(jnp.where(same, dot(member, earlier), 0.0), axis=0, keepdims=True)
    homes = jnp.broadcast_to(home_of[...].astype(F32), (8, 128)).astype(BF)
    home = dot(homes, member)[0:1]
    row = iota((8, 512), 0)
    pair = jnp.where(row == 0, home, jnp.where(row == 1, ordinal, 0.0)).astype(BF)
    for o in range(2):
        chosen = onehot(iota((512, 512), 0) == target_of[o : o + 1, :])
        picked = dot(pair, chosen)
        slots[o : o + 1, :] = (picked[0:1] * SLOTS + picked[1:2]).astype(I32)
    to_home = onehot(iota((128, 512), 0) == home.astype(I32))
    lane = ordinal.astype(I32) + SLOTS * lax.rem(me, 8)
    at_lane = iota((128, 512), 0) == lane
    block = block_of[...]
    upper = jnp.where(at_lane, (block // 16).astype(F32), 0.0).astype(BF)
    lower = jnp.where(at_lane, (block % 16).astype(F32), 0.0).astype(BF)
    block_rows[...] = dot_nt(to_home, upper) * 16.0 + dot_nt(to_home, lower)


def middle_eigen(j00, j01, j02, j10, j11, j12, j20, j21, j22):
    p01 = j01 * j10
    p02 = j02 * j20
    p12 = j12 * j21
    m00 = j00 * j00 + p01 + p02
    m11 = j11 * j11 + p01 + p12
    m22 = j22 * j22 + p02 + p12
    m01 = 0.5 * ((j00 + j11) * (j01 + j10) + j02 * j21 + j12 * j20)
    m02 = 0.5 * ((j00 + j22) * (j02 + j20) + j01 * j12 + j21 * j10)
    m12 = 0.5 * ((j11 + j22) * (j12 + j21) + j10 * j02 + j20 * j01)
    q = (m00 + m11 + m22) * (1.0 / 3.0)
    a00 = m00 - q
    a11 = m11 - q
    a22 = m22 - q
    s01 = m01 * m01
    s02 = m02 * m02
    s12 = m12 * m12
    s = (a00 * a00 + a11 * a11 + a22 * a22) * (1.0 / 6.0) + (s01 + s02 + s12) * (1.0 / 3.0)
    det = a00 * (a11 * a22 - s12) - a11 * s02 - a22 * s01 + 2.0 * (m01 * m02 * m12)
    h = 0.5 * det
    root = jnp.sqrt(s)
    disc = jnp.maximum(s * s * s - h * h, 0.0)
    z = h / jnp.maximum(s * root + jnp.sqrt(disc), 1e-37)
    w = z * z
    poly = SINE_POLY[-1]
    for coefficient in SINE_POLY[-2::-1]:
        poly = poly * w + coefficient
    return q - 2.0 * root * (z * poly)


def stitch_plane(grad, layer, base):
    lane = iota((8, CROSS), 1)
    normal = lane // EZN
    span = lane % EZN
    for m in range(9):
        view = grad.at[layer, m]
        first = view[pl.ds(base, 8), :]
        last = view[pl.ds(base + 56, 8), :]
        view[pl.ds(base, 8), :] = jnp.where(
            normal > 0, 0.5 * (first + pltpu.roll(last, EZN, 1)), first
        )
        view[pl.ds(base + 56, 8), :] = jnp.where(
            normal < EYN - 1, 0.5 * (last + pltpu.roll(first, CROSS - EZN, 1)), last
        )
    for m in range(9):
        view = grad.at[layer, m]
        first = view[pl.ds(base, 8, stride=8), :]
        last = view[pl.ds(base + 7, 8, stride=8), :]
        before = jnp.where(
            span == 0, pltpu.roll(last, CROSS + 1 - EZN, 1), pltpu.roll(last, 1, 1)
        )
        after = jnp.where(
            span == EZN - 1, pltpu.roll(first, EZN - 1, 1), pltpu.roll(first, CROSS - 1, 1)
        )
        view[pl.ds(base, 8, stride=8), :] = 0.5 * (first + before)
        view[pl.ds(base + 7, 8, stride=8), :] = 0.5 * (last + after)


def resample(layer, o, lam, res_x, res_y, res_z, rows, stage_z, stage_y):
    lanes = pl.ds(pl.multiple_of(layer * CROSS, CROSS), CROSS)

    def along_z(i, carry):
        base = i * 64
        points = [lam[layer, pl.ds(base + k, 8, stride=8), :] for k in range(8)]
        for w in range(4):
            total = points[0] * res_z[o, w, 0:1, lanes]
            for k in range(1, 8):
                total = total + points[k] * res_z[o, w, k : k + 1, lanes]
            stage_z[pl.ds(pl.multiple_of(w * 64 + i * 8, 8), 8), :] = total
        return carry

    lax.fori_loop(0, 8, along_z, 0)
    for w in range(4):
        points = [stage_z[pl.ds(w * 64 + j, 8, stride=8), :] for j in range(8)]
        for v in range(4):
            total = points[0] * res_y[o, v, 0:1, lanes]
            for j in range(1, 8):
                total = total + points[j] * res_y[o, v, j : j + 1, lanes]
            stage_y[32 * v + 8 * w : 32 * v + 8 * w + 8, :] = total
    points = [
        jnp.concatenate(
            [stage_y[pl.ds(i, 8, stride=8), :], stage_y[pl.ds(64 + i, 8, stride=8), :]], axis=0
        )
        for i in range(8)
    ]
    at = pl.ds(pl.multiple_of(o * 512 + layer * CROSS, CROSS), CROSS)
    for u in range(8):
        total = points[0] * res_x[o, u, 0:1, lanes]
        for i in range(1, 8):
            total = total + points[i] * res_x[o, u, i : i + 1, lanes]
        upper = total.astype(BF)
        rows[16 * u : 16 * u + 16, at] = upper
        rows[128 + 16 * u : 144 + 16 * u, at] = (total - upper.astype(F32)).astype(BF)


def front_kernel(
    vel_h, face_op_h, inv_h, op_x_h, op_yz_h, target_h, brick_h, block_h, home_h, x_h, y_h, z_h,
    rows, slots, block_rows,
    vel, face_op, inv, op_x, op_yz, target_of, brick_of, block_of, home_of, res_x, res_y, res_z,
    rims, halo, grad, lam, stage_z, stage_y, load_sems, send_sems, recv_sems,
):
    me = lax.axis_index("dom")
    count = lax.axis_size("dom")
    after, before = lax.rem(me + 1, count), lax.rem(me + count - 1, count)
    barrier = pltpu.get_barrier_semaphore()
    for peer in (before, after):
        pl.semaphore_signal(barrier, inc=1, device_id=(peer,), device_id_type=pl.DeviceIdType.MESH)
    remote = (vel_h, face_op_h, inv_h, op_x_h, op_yz_h, target_h, brick_h, block_h, home_h, x_h, y_h, z_h)
    local = (vel, face_op, inv, op_x, op_yz, target_of, brick_of, block_of, home_of, res_x, res_y, res_z)
    loads = [pltpu.make_async_copy(r, l, load_sems.at[n]) for n, (r, l) in enumerate(zip(remote, local))]
    for load in loads:
        load.start()

    for load in loads[:3]:
        load.wait()
    for side, layer in ((0, 0), (1, LAYERS - 1)):
        lanes = slice(CROSS * layer, CROSS * layer + CROSS)
        columns = jnp.concatenate([vel[c, :, lanes] for c in range(3)], axis=1)
        faces = dot(face_op[192 * side : 192 * side + 192, :], columns)
        for c in range(3):
            for a in range(3):
                part = faces[64 * a : 64 * a + 64, CROSS * c : CROSS * c + CROSS]
                rims[side, 3 * c + a] = part * inv[a : a + 1, lanes]

    for load in loads[5:9]:
        load.wait()
    route(target_of, brick_of, block_of, home_of, slots, block_rows)

    pl.semaphore_wait(barrier, 2)
    sends = [
        pltpu.make_async_remote_copy(
            src_ref=rims.at[side], dst_ref=halo.at[1 - side],
            send_sem=send_sems.at[side], recv_sem=recv_sems.at[1 - side],
            device_id=(peer,), device_id_type=pl.DeviceIdType.MESH,
        )
        for side, peer in ((0, before), (1, after))
    ]
    for send in sends:
        send.start()

    for load in loads[3:5]:
        load.wait()
    for c in range(3):
        along_x = dot(op_x[...], vel[c])
        for layer in range(LAYERS):
            lanes = slice(CROSS * layer, CROSS * layer + CROSS)
            grad[layer, 3 * c] = along_x[:, lanes] * inv[0:1, lanes]
        for half in range(2):
            both = dot(op_yz[...], vel[c, 256 * half : 256 * half + 256, :])
            for a in (1, 2):
                for layer in range(LAYERS):
                    lanes = slice(CROSS * layer, CROSS * layer + CROSS)
                    grad[layer, 3 * c + a, 256 * half : 256 * half + 256, :] = (
                        both[256 * a - 256 : 256 * a, lanes] * inv[a : a + 1, lanes]
                    )
    for layer in range(LAYERS - 1):
        for m in range(9):
            mean = 0.5 * (grad[layer, m, 448:512, :] + grad[layer + 1, m, 0:64, :])
            grad[layer, m, 448:512, :] = mean
            grad[layer + 1, m, 0:64, :] = mean

    def plane_of(layer_of):
        def plane(t, carry):
            layer = layer_of(t // 8)
            base = pl.multiple_of(lax.rem(t, 8) * 64, 64)
            stitch_plane(grad, layer, base)
            for j in range(8):
                at = pl.ds(base + 8 * j, 8)
                lam[layer, at, :] = middle_eigen(*[grad[layer, m, at, :] for m in range(9)])
            return carry

        return plane

    def resample_of(layer_of):
        def both(n, carry):
            for o in range(2):
                resample(layer_of(n), o, lam, res_x, res_y, res_z, rows, stage_z, stage_y)
            return carry

        return both

    lax.fori_loop(0, 16, plane_of(lambda n: n + 1), 0)
    for load in loads[9:]:
        load.wait()
    lax.fori_loop(0, 2, resample_of(lambda n: n + 1), 0)
    for send in sends:
        send.wait_recv()
    for m in range(9):
        grad[0, m, 0:64, :] = 0.5 * (grad[0, m, 0:64, :] + halo[0, m])
        grad[LAYERS - 1, m, 448:512, :] = 0.5 * (grad[LAYERS - 1, m, 448:512, :] + halo[1, m])
    lax.fori_loop(0, 16, plane_of(lambda n: n * (LAYERS - 1)), 0)
    lax.fori_loop(0, 2, resample_of(lambda n: n * (LAYERS - 1)), 0)
    for send in sends:
        send.wait_send()


def back_kernel(rows, slots, block_rows, bricks, source, landed, send_sem, recv_sems, own_sem):
    me = lax.axis_index("dom")
    count = lax.axis_size("dom")
    mine = me // 16
    barrier = pltpu.get_barrier_semaphore()

    def greet(step, carry):
        pl.semaphore_signal(
            barrier, inc=1, device_id=(lax.rem(me + step, count),),
            device_id_type=pl.DeviceIdType.MESH,
        )
        return carry

    lax.fori_loop(1, count, greet, 0)
    slot_row = jnp.concatenate([slots[0:1, :], slots[1:2, :]], axis=1)

    def pack(g, carry):
        base = pl.multiple_of(g * 16, 16)
        chosen = onehot(iota((256, 1024), 0) + g * 256 == slot_row)
        packed = dot_nt(chosen, rows[...])
        source[pl.ds(base, 16), 0:SLOTS, :] = (packed[:, 0:128] + packed[:, 128:256]).reshape(16, SLOTS, 128)
        source[pl.ds(base, 16), SLOTS, :] = block_rows[pl.ds(base, 16), :]
        return carry

    lax.fori_loop(0, 8, pack, 0)
    pl.semaphore_wait(barrier, count - 1)

    def push(step, carry):
        peer = lax.rem(me + step, count)
        pltpu.make_async_remote_copy(
            src_ref=source.at[peer], dst_ref=landed.at[me], send_sem=send_sem, recv_sem=recv_sems.at[mine],
            device_id=(peer,), device_id_type=pl.DeviceIdType.MESH,
        ).start()
        return carry

    lax.fori_loop(1, count, push, 0)
    own = pltpu.make_async_copy(source.at[me], landed.at[me], own_sem)
    own.start()
    own.wait()

    def arrived(chunk, number):
        part = landed.at[pl.ds(0, number)]
        pltpu.make_async_remote_copy(
            src_ref=part, dst_ref=part, send_sem=send_sem, recv_sem=recv_sems.at[chunk],
            device_id=(me,), device_id_type=pl.DeviceIdType.MESH,
        ).wait_recv()

    def unpack(chunk, first):
        base = pl.multiple_of(chunk * 16, 16)
        block = jnp.sum(landed[pl.ds(base, 16), SLOTS, :].reshape(2, 8, 128), axis=1).astype(I32)
        named = jnp.concatenate([block[0:1], block[1:2]], axis=1)
        values = landed[pl.ds(base, 16), 0:SLOTS, :].reshape(256, 128)
        upper = values.astype(BF)
        lower = (values - upper.astype(F32)).astype(BF)
        both = jnp.concatenate([upper, lower], axis=1)
        for part in range(8):
            term = dot(onehot(iota((256, 256), 0) + 256 * part == named), both)
            term = term[:, 0:128] + term[:, 128:256]
            at = slice(256 * part, 256 * part + 256)
            bricks[0, at, :] = term if first else bricks[0, at, :] + term

    arrived(mine, 15)
    unpack(mine, True)

    def receive(step, carry):
        chunk = lax.rem(mine + 8 - step, 8)
        arrived(chunk, 16)
        unpack(chunk, False)
        return carry

    lax.fori_loop(1, 8, receive, 0)
    everything = source.at[pl.ds(0, count - 1)]
    pltpu.make_async_remote_copy(
        src_ref=everything, dst_ref=everything, send_sem=send_sem, recv_sem=recv_sems.at[0],
        device_id=(me,), device_id_type=pl.DeviceIdType.MESH,
    ).wait_send()


ANYWHERE = pl.BlockSpec(memory_space=pl.ANY)
IN_VMEM = pl.BlockSpec(memory_space=pltpu.VMEM)


def operators():
    d = diff_matrix()
    one = np.eye(8)
    op_x = np.kron(np.kron(d, one), one)
    op_y = np.kron(np.kron(one, d), one)
    op_z = np.kron(np.kron(one, one), d)
    face = np.concatenate([op[rows] for rows in (slice(0, 64), slice(448, 512)) for op in (op_x, op_y, op_z)])
    op_yz = np.concatenate([op_y[:256, :256], op_z[:256, :256]])
    return [jnp.asarray(op, F32).astype(BF) for op in (face, op_x, op_yz)]


def front(velocity, inverse_sizes, resample_x, resample_y, resample_z, piece_target, target_brick, target_block, brick_home):
    face_op, op_x, op_yz = operators()
    operands = (
        velocity, face_op, inverse_sizes, op_x, op_yz,
        piece_target, target_brick.reshape(1, 512), target_block.reshape(1, 512), brick_home.reshape(1, 128),
        resample_x, resample_y, resample_z,
    )
    scratch = [pltpu.VMEM(array.shape, array.dtype) for array in operands]
    scratch += [
        pltpu.VMEM((2, 9, 64, 128), F32),
        pltpu.VMEM((2, 9, 64, 128), F32),
        pltpu.VMEM((LAYERS, 9, 512, 128), F32),
        pltpu.VMEM((LAYERS, 512, 128), F32),
        pltpu.VMEM((256, 128), F32),
        pltpu.VMEM((128, 128), F32),
        pltpu.SemaphoreType.DMA((len(operands),)),
        pltpu.SemaphoreType.DMA((2,)),
        pltpu.SemaphoreType.DMA((2,)),
    ]
    return pl.pallas_call(
        front_kernel,
        in_specs=[ANYWHERE] * len(operands),
        out_specs=(IN_VMEM,) * 3,
        out_shape=(
            jax.ShapeDtypeStruct((256, 1024), BF),
            jax.ShapeDtypeStruct((2, 512), I32),
            jax.ShapeDtypeStruct((128, 128), F32),
        ),
        scratch_shapes=scratch,
        compiler_params=pltpu.CompilerParams(collective_id=0, has_side_effects=True),
        name="front",
    )(*operands)


def back(rows, slots, block_rows):
    buffer = pltpu.VMEM((128, SLOTS + 1, 128), F32)
    return pl.pallas_call(
        back_kernel,
        in_specs=[IN_VMEM] * 3,
        out_specs=IN_VMEM,
        out_shape=jax.ShapeDtypeStruct((1, BLOCKS, 128), F32),
        scratch_shapes=[
            buffer, buffer, pltpu.SemaphoreType.DMA, pltpu.SemaphoreType.DMA((8,)), pltpu.SemaphoreType.DMA,
        ],
        compiler_params=pltpu.CompilerParams(collective_id=1, has_side_effects=True),
        name="back",
    )(rows, slots, block_rows)


def shards(*operands):
    return back(*front(*operands))


def solution(mesh):
    return jax.shard_map(
        shards,
        mesh=mesh,
        in_specs=(
            P(None, None, "dom"),
            P(None, "dom"),
            P(None, None, None, "dom"),
            P(None, None, None, "dom"),
            P(None, None, None, "dom"),
            P(None, "dom"),
            P("dom", None),
            P("dom"),
            P(),
        ),
        out_specs=P("dom", None, None),
        check_vma=False,
    )
```

```python
import math

import jax
import jax.numpy as jnp
import numpy as np
from jax import lax
from jax.experimental import pallas as pl
from jax.experimental.pallas import tpu as pltpu
from jax.sharding import PartitionSpec as P

EYN = 8
EZN = 16
BLOCKS = 2048
CROSS = 128
LAYERS = 4
SLOTS = 16
BF = jnp.bfloat16
F32 = jnp.float32
I32 = jnp.int32
VMEM_LIMIT = 60 * 1024 * 1024

GLL_NODES = [
    -1.0,
    -0.8717401485096066,
    -0.5917001814331423,
    -0.2092992179024789,
    0.2092992179024789,
    0.5917001814331423,
    0.8717401485096066,
    1.0,
]

THIRD_POLY = (
    0.28867512941360474,
    -0.16666603088378906,
    0.12827838957309723,
    -0.10773465782403946,
    0.09301131963729858,
    -0.0773678869009018,
    0.0560062974691391,
    -0.03085879236459732,
    0.010898211039602757,
    -0.0017919066594913602,
)


def diff_matrix():
    nodes = GLL_NODES
    weights = []
    for first in range(8):
        product_term = 1.0
        for other in range(8):
            if other != first:
                product_term = product_term * (nodes[first] - nodes[other])
        weights.append(1.0 / product_term)
    rows = []
    for first in range(8):
        row = []
        for second in range(8):
            if second == first:
                row.append(0.0)
            else:
                row.append(weights[second] / weights[first] / (nodes[first] - nodes[second]))
        row[first] = -sum(row)
        rows.append(row)
    return np.array(rows)


def iota(shape, dim):
    return lax.broadcasted_iota(I32, shape, dim)


def onehot(mask):
    return jnp.where(mask, 1.0, 0.0).astype(BF)


def dot(a, b):
    return jnp.dot(a, b, preferred_element_type=F32)


def dot_nt(a, b):
    return lax.dot_general(a, b, (((1,), (1,)), ((), ())), preferred_element_type=F32)


def route(target_of, brick_of, block_of, home_of, slots, block_rows):
    me = lax.axis_index("dom")
    same = iota((128, 512), 0) == brick_of[...]
    member = onehot(same)
    earlier = onehot(iota((512, 512), 0) < iota((512, 512), 1))
    ordinal = jnp.sum(jnp.where(same, dot(member, earlier), 0.0), axis=0, keepdims=True)
    homes = jnp.broadcast_to(home_of[...].astype(F32), (8, 128)).astype(BF)
    home = dot(homes, member)[0:1]
    row = iota((8, 512), 0)
    pair = jnp.where(row == 0, home, jnp.where(row == 1, ordinal, 0.0)).astype(BF)
    for o in range(2):
        chosen = onehot(iota((512, 512), 0) == target_of[o : o + 1, :])
        picked = dot(pair, chosen)
        slots[o : o + 1, :] = (picked[0:1] * SLOTS + picked[1:2]).astype(I32)
    to_home = onehot(iota((128, 512), 0) == home.astype(I32))
    lane = ordinal.astype(I32) + SLOTS * lax.rem(me, 8)
    at_lane = iota((128, 512), 0) == lane
    block = block_of[...]
    upper = jnp.where(at_lane, (block // 16).astype(F32), 0.0).astype(BF)
    lower = jnp.where(at_lane, (block % 16).astype(F32), 0.0).astype(BF)
    block_rows[...] = dot_nt(to_home, upper) * 16.0 + dot_nt(to_home, lower)


def middle_eigen(j00, j01, j02, j10, j11, j12, j20, j21, j22):
    p01 = j01 * j10
    p02 = j02 * j20
    p12 = j12 * j21
    m00 = j00 * j00 + (p01 + p02)
    m11 = j11 * j11 + (p01 + p12)
    m22 = j22 * j22 + (p02 + p12)
    n01 = (j00 + j11) * (j01 + j10) + (j02 * j21 + j12 * j20)
    n02 = (j00 + j22) * (j02 + j20) + (j01 * j12 + j21 * j10)
    n12 = (j11 + j22) * (j12 + j21) + (j10 * j02 + j20 * j01)
    q = (m00 + m11 + m22) * (1.0 / 3.0)
    a00 = m00 - q
    a11 = m11 - q
    a22 = m22 - q
    s01 = n01 * n01
    s02 = n02 * n02
    s12 = n12 * n12
    a00x2 = a00 + a00
    minor = 4.0 * a11 * a22
    s_12 = (a00x2 * a00x2 - minor) + (s01 + s02 + s12)
    det_4 = a00 * (minor - s12) - (a11 * s02 + a22 * s01) + n01 * n02 * n12
    s_12 = jnp.maximum(s_12, 1e-24)
    inverse = lax.rsqrt(s_12)
    ratio = (det_4 * (3.0 * math.sqrt(3.0))) * (inverse * inverse * inverse)
    rest = jnp.maximum(1.0 - ratio * ratio, 1e-30)
    cosine = rest * lax.rsqrt(rest)
    poly = THIRD_POLY[-1]
    for coefficient in THIRD_POLY[-2::-1]:
        poly = poly * cosine + coefficient
    return q - (s_12 * inverse) * (ratio * poly)


def stitch_y(first, last):
    normal = iota((8, CROSS), 1) // EZN
    return (
        jnp.where(normal > 0, 0.5 * (first + pltpu.roll(last, EZN, 1)), first),
        jnp.where(normal < EYN - 1, 0.5 * (last + pltpu.roll(first, CROSS - EZN, 1)), last),
    )


def stitch_z(first, last):
    span = iota((8, CROSS), 1) % EZN
    before = jnp.where(span == 0, pltpu.roll(last, CROSS + 1 - EZN, 1), pltpu.roll(last, 1, 1))
    after = jnp.where(
        span == EZN - 1, pltpu.roll(first, EZN - 1, 1), pltpu.roll(first, CROSS - 1, 1)
    )
    return 0.5 * (first + before), 0.5 * (last + after)


def stitch_plane(grad, layer, firsts, lasts, stitch):
    pairs = [(grad[layer, m, firsts, :], grad[layer, m, lasts, :]) for m in range(9)]
    pairs = [stitch(first, last) for first, last in pairs]
    for m in range(9):
        grad[layer, m, firsts, :] = pairs[m][0]
        grad[layer, m, lasts, :] = pairs[m][1]


def stitch_plane_z(grad, layer, base):
    stitch_plane(grad, layer, pl.ds(base, 8, stride=8), pl.ds(base + 7, 8, stride=8), stitch_z)


def eigen_plane(grad, lam, layer, base):
    for j in range(8):
        at = pl.ds(base + 8 * j, 8)
        lam[layer, at, :] = middle_eigen(*[grad[layer, m, at, :] for m in range(9)])


def resample(layer, o, lam, res_x, res_y, res_z, rows, stage_z, stage_y):
    lanes = pl.ds(pl.multiple_of(layer * CROSS, CROSS), CROSS)

    def along_z(i, carry):
        base = i * 64
        points = [lam[layer, pl.ds(base + k, 8, stride=8), :] for k in range(8)]
        for w in range(4):
            total = points[0] * res_z[o, w, 0:1, lanes]
            for k in range(1, 8):
                total = total + points[k] * res_z[o, w, k : k + 1, lanes]
            stage_z[pl.ds(pl.multiple_of(w * 64 + i * 8, 8), 8), :] = total
        return carry

    lax.fori_loop(0, 8, along_z, 0)
    for w in range(4):
        points = [stage_z[pl.ds(w * 64 + j, 8, stride=8), :] for j in range(8)]
        for v in range(4):
            total = points[0] * res_y[o, v, 0:1, lanes]
            for j in range(1, 8):
                total = total + points[j] * res_y[o, v, j : j + 1, lanes]
            stage_y[32 * v + 8 * w : 32 * v + 8 * w + 8, :] = total
    points = [
        jnp.concatenate(
            [stage_y[pl.ds(i, 8, stride=8), :], stage_y[pl.ds(64 + i, 8, stride=8), :]], axis=0
        )
        for i in range(8)
    ]
    at = pl.ds(pl.multiple_of(o * 512 + layer * CROSS, CROSS), CROSS)
    for u in range(8):
        total = points[0] * res_x[o, u, 0:1, lanes]
        for i in range(1, 8):
            total = total + points[i] * res_x[o, u, i : i + 1, lanes]
        upper = total.astype(BF)
        rows[16 * u : 16 * u + 16, at] = upper
        rows[128 + 16 * u : 144 + 16 * u, at] = (total - upper.astype(F32)).astype(BF)


def differentiate(vel, op_x, op_yz, inv, grad, rims):
    for c in range(3):
        along_x = dot(op_x[...], vel[c])
        halves = [dot(op_yz[...], vel[c, 256 * half : 256 * half + 256, :]) for half in range(2)]
        for a in range(3):
            m = 3 * c + a

            def block(i, layer, a=a):
                lanes = slice(CROSS * layer, CROSS * layer + CROSS)
                if a == 0:
                    rows = along_x[64 * i : 64 * i + 64, lanes]
                else:
                    at = 256 * (a - 1) + 64 * (i % 4)
                    rows = halves[i // 4][at : at + 64, lanes]
                return rows * inv[a : a + 1, lanes]

            rims[0, m] = block(0, 0)
            rims[1, m] = block(7, LAYERS - 1)
            for layer in range(LAYERS):
                for i in range(1, 8):
                    if i == 7 and layer == LAYERS - 1:
                        continue
                    values = block(i, layer)
                    if i == 7:
                        values = 0.5 * (values + block(0, layer + 1))
                    first, last = stitch_y(values[0:8], values[56:64])
                    places = [(layer, 64 * i)] + ([(layer + 1, 0)] if i == 7 else [])
                    for place, base in places:
                        grad[place, m, base : base + 8, :] = first
                        grad[place, m, base + 8 : base + 56, :] = values[8:56]
                        grad[place, m, base + 56 : base + 64, :] = last


def kernel(
    vel_h, inv_h, op_x_h, op_yz_h, target_h, brick_h, block_h, home_h, x_h, y_h, z_h,
    bricks,
    vel, inv, op_x, op_yz, target_of, brick_of, block_of, home_of, res_x, res_y, res_z,
    rims, halo, grad, lam, stage_z, stage_y, rows, slots, block_rows, source, landed,
    load_sems, halo_send, halo_recv, send_sem, recv_sems, own_sem,
):
    me = lax.axis_index("dom")
    count = lax.axis_size("dom")
    mine = me // 16
    mesh_id = pl.DeviceIdType.MESH

    far = (vel_h, inv_h, op_x_h, op_yz_h, target_h, brick_h, block_h, home_h, x_h, y_h, z_h)
    near = (vel, inv, op_x, op_yz, target_of, brick_of, block_of, home_of, res_x, res_y, res_z)
    loads = [pltpu.make_async_copy(f, n, load_sems.at[k]) for k, (f, n) in enumerate(zip(far, near))]
    for load in loads:
        load.start()
    barrier = pltpu.get_barrier_semaphore()

    def greet(step, carry):
        pl.semaphore_signal(
            barrier, inc=1, device_id=(lax.rem(me + step, count),), device_id_type=mesh_id
        )
        return carry

    lax.fori_loop(1, count, greet, 0)
    for load in loads[:4]:
        load.wait()
    differentiate(vel, op_x, op_yz, inv, grad, rims)

    def plane_z(t, carry):
        stitch_plane_z(grad, t // 8, pl.multiple_of(lax.rem(t, 8) * 64, 64))
        return carry

    def plane_eigen(t, carry):
        eigen_plane(grad, lam, t // 8, pl.multiple_of(lax.rem(t, 8) * 64, 64))
        return carry

    lax.fori_loop(1, 31, plane_z, 0)
    for load in loads[4:8]:
        load.wait()
    route(target_of, brick_of, block_of, home_of, slots, block_rows)

    pl.semaphore_wait(barrier, count - 1)
    sends = [
        pltpu.make_async_remote_copy(
            src_ref=rims.at[side], dst_ref=halo.at[1 - side],
            send_sem=halo_send.at[side], recv_sem=halo_recv.at[1 - side],
            device_id=(lax.rem(me + step, count),), device_id_type=mesh_id,
        )
        for side, step in ((0, count - 1), (1, 1))
    ]
    for send in sends:
        send.start()

    lax.fori_loop(1, 31, plane_eigen, 0)
    for load in loads[8:]:
        load.wait()

    def resample_of(layer_of):
        def both(n, carry):
            for o in range(2):
                resample(layer_of(n), o, lam, res_x, res_y, res_z, rows, stage_z, stage_y)
            return carry

        return both

    lax.fori_loop(0, 2, resample_of(lambda n: n + 1), 0)
    for send in sends:
        send.wait_recv()
    for side, layer, base in ((0, 0, 0), (1, LAYERS - 1, 448)):
        for m in range(9):
            grad[layer, m, base : base + 64, :] = 0.5 * (rims[side, m] + halo[side, m])
        stitch_plane(grad, layer, slice(base, base + 8), slice(base + 56, base + 64), stitch_y)
    for layer, base in ((0, 0), (LAYERS - 1, 448)):
        stitch_plane_z(grad, layer, base)
    for layer, base in ((0, 0), (LAYERS - 1, 448)):
        eigen_plane(grad, lam, layer, base)
    lax.fori_loop(0, 2, resample_of(lambda n: n * (LAYERS - 1)), 0)

    slot_row = jnp.concatenate([slots[0:1, :], slots[1:2, :]], axis=1)

    def push(chunk, first):
        def one(step, carry):
            peer = chunk * 16 + lax.rem(me + step, 16)
            pltpu.make_async_remote_copy(
                src_ref=source.at[peer], dst_ref=landed.at[me],
                send_sem=send_sem, recv_sem=recv_sems.at[mine],
                device_id=(peer,), device_id_type=mesh_id,
            ).start()
            return carry

        lax.fori_loop(first, 16, one, 0)

    def pack(g, carry):
        chunk = lax.rem(mine + 1 + g, 8)
        base = pl.multiple_of(chunk * 16, 16)
        chosen = onehot(iota((256, 1024), 0) + chunk * 256 == slot_row)
        packed = dot_nt(chosen, rows[...])
        source[pl.ds(base, 16), 0:SLOTS, :] = (packed[:, 0:128] + packed[:, 128:256]).reshape(16, SLOTS, 128)
        source[pl.ds(base, 16), SLOTS, :] = block_rows[pl.ds(base, 16), :]

        @pl.when(g > 0)
        def _():
            push(lax.rem(mine + g, 8), 0)

        return carry

    lax.fori_loop(0, 8, pack, 0)
    for send in sends:
        send.wait_send()
    push(mine, 1)
    own = pltpu.make_async_copy(source.at[me], landed.at[me], own_sem)
    own.start()
    own.wait()

    def arrived(chunk, number):
        part = landed.at[pl.ds(0, number)]
        pltpu.make_async_remote_copy(
            src_ref=part, dst_ref=part, send_sem=send_sem, recv_sem=recv_sems.at[chunk],
            device_id=(me,), device_id_type=mesh_id,
        ).wait_recv()

    def unpack(chunk):
        base = pl.multiple_of(chunk * 16, 16)
        block = jnp.sum(landed[pl.ds(base, 16), SLOTS, :].reshape(2, 8, 128), axis=1).astype(I32)
        named = jnp.concatenate([block[0:1], block[1:2]], axis=1)
        values = landed[pl.ds(base, 16), 0:SLOTS, :].reshape(256, 128)
        upper = values.astype(BF)
        lower = (values - upper.astype(F32)).astype(BF)
        both = jnp.concatenate([upper, lower], axis=1)
        for part in range(8):
            term = dot(onehot(iota((256, 256), 0) + 256 * part == named), both)
            at = slice(256 * part, 256 * part + 256)
            bricks[0, at, :] += term[:, 0:128] + term[:, 128:256]

    bricks[...] = jnp.zeros_like(bricks)

    def receive(g, carry):
        chunk = lax.rem(mine + 7 - g, 8)
        arrived(chunk, 16)
        unpack(chunk)
        return carry

    lax.fori_loop(0, 7, receive, 0)
    arrived(mine, 15)
    unpack(mine)
    everything = source.at[pl.ds(0, count - 1)]
    pltpu.make_async_remote_copy(
        src_ref=everything, dst_ref=everything, send_sem=send_sem, recv_sem=recv_sems.at[0],
        device_id=(me,), device_id_type=mesh_id,
    ).wait_send()


def operators():
    d = diff_matrix()
    one = np.eye(8)
    op_x = np.kron(np.kron(d, one), one)
    op_y = np.kron(np.kron(np.eye(4), d), one)
    op_z = np.kron(np.eye(32), d)
    return [jnp.asarray(op, F32).astype(BF) for op in (op_x, np.concatenate([op_y, op_z]))]


def shards(velocity, inverse_sizes, resample_x, resample_y, resample_z, piece_target, target_brick, target_block, brick_home):
    op_x, op_yz = operators()
    operands = (
        velocity, inverse_sizes, op_x, op_yz,
        piece_target, target_brick.reshape(1, 512), target_block.reshape(1, 512), brick_home.reshape(1, 128),
        resample_x, resample_y, resample_z,
    )
    scratch = [pltpu.VMEM(array.shape, array.dtype) for array in operands]
    scratch += [
        pltpu.VMEM((2, 9, 64, 128), F32),
        pltpu.VMEM((2, 9, 64, 128), F32),
        pltpu.VMEM((LAYERS, 9, 512, 128), F32),
        pltpu.VMEM((LAYERS, 512, 128), F32),
        pltpu.VMEM((256, 128), F32),
        pltpu.VMEM((128, 128), F32),
        pltpu.VMEM((256, 1024), BF),
        pltpu.VMEM((2, 512), I32),
        pltpu.VMEM((128, 128), F32),
        pltpu.VMEM((128, SLOTS + 1, 128), F32),
        pltpu.VMEM((128, SLOTS + 1, 128), F32),
        pltpu.SemaphoreType.DMA((len(operands),)),
        pltpu.SemaphoreType.DMA((2,)),
        pltpu.SemaphoreType.DMA((2,)),
        pltpu.SemaphoreType.DMA,
        pltpu.SemaphoreType.DMA((8,)),
        pltpu.SemaphoreType.DMA,
    ]
    return pl.pallas_call(
        kernel,
        in_specs=[pl.BlockSpec(memory_space=pltpu.HBM)] * len(operands),
        out_specs=pl.BlockSpec(memory_space=pltpu.VMEM),
        out_shape=jax.ShapeDtypeStruct((1, BLOCKS, 128), F32),
        scratch_shapes=scratch,
        compiler_params=pltpu.CompilerParams(
            collective_id=0, has_side_effects=True, vmem_limit_bytes=VMEM_LIMIT
        ),
        name="step",
    )(*operands)


def solution(mesh):
    return jax.shard_map(
        shards,
        mesh=mesh,
        in_specs=(
            P(None, None, "dom"),
            P(None, "dom"),
            P(None, None, None, "dom"),
            P(None, None, None, "dom"),
            P(None, None, None, "dom"),
            P(None, "dom"),
            P("dom", None),
            P("dom"),
            P(),
        ),
        out_specs=P("dom", None, None),
        check_vma=False,
    )
```

```python
import math

import jax
import jax.numpy as jnp
import numpy as np
from jax import lax
from jax.experimental import pallas as pl
from jax.experimental.pallas import tpu as pltpu
from jax.sharding import PartitionSpec as P

EYN = 8
EZN = 16
BLOCKS = 2048
CROSS = 128
LAYERS = 4
SLOTS = 16
BF = jnp.bfloat16
F32 = jnp.float32
I32 = jnp.int32
VMEM_LIMIT = 40 << 20

GLL_NODES = [
    -1.0,
    -0.8717401485096066,
    -0.5917001814331423,
    -0.2092992179024789,
    0.2092992179024789,
    0.5917001814331423,
    0.8717401485096066,
    1.0,
]

THIRD_POLY = (
    0.28867512941360474,
    -0.16666603088378906,
    0.12827838957309723,
    -0.10773465782403946,
    0.09301131963729858,
    -0.0773678869009018,
    0.0560062974691391,
    -0.03085879236459732,
    0.010898211039602757,
    -0.0017919066594913602,
)


def far_first():
    hops = (0, 1, 2, 1)
    offsets = [np.unravel_index(n, (4, 4, 4, 2)) for n in np.random.RandomState(1).permutation(128)]
    offsets.sort(key=lambda at: (any(at) == 0, -hops[at[0]] - hops[at[1]] - hops[at[2]]))
    return [tuple(int(part) for part in at) for at in offsets]


OFFSETS = far_first()
PACKS = ((0, 2), (2, 2), (4, 2), (6, 2))
GROUPS = ((0, 2), (2, 2), (4, 2), (6, 2))


def diff_matrix():
    nodes = GLL_NODES
    weights = []
    for first in range(8):
        product_term = 1.0
        for other in range(8):
            if other != first:
                product_term = product_term * (nodes[first] - nodes[other])
        weights.append(1.0 / product_term)
    rows = []
    for first in range(8):
        row = []
        for second in range(8):
            if second == first:
                row.append(0.0)
            else:
                row.append(weights[second] / weights[first] / (nodes[first] - nodes[second]))
        row[first] = -sum(row)
        rows.append(row)
    return np.array(rows)


def iota(shape, dim):
    return lax.broadcasted_iota(I32, shape, dim)


def onehot(mask):
    return jnp.where(mask, 1.0, 0.0).astype(BF)


def dot(a, b):
    return jnp.dot(a, b, preferred_element_type=F32)


def dot_nt(a, b):
    return lax.dot_general(a, b, (((1,), (1,)), ((), ())), preferred_element_type=F32)


def torus(index):
    return index // 32, (index // 8) % 4, (index // 2) % 4, index % 2


def route(ranks, target_of, brick_of, block_of, home_of, slots, block_rows):
    here = torus(lax.axis_index("dom"))
    same = iota((128, 512), 0) == brick_of[...]
    member = onehot(same)
    earlier = onehot(iota((512, 512), 0) < iota((512, 512), 1))
    ordinal = jnp.sum(jnp.where(same, dot(member, earlier), 0.0), axis=0, keepdims=True)
    homes = jnp.broadcast_to(home_of[...].astype(F32), (8, 128)).astype(BF)
    there = torus(dot(homes, member)[0:1].astype(I32))
    away = [(there[k] - here[k] + size) % size for k, size in enumerate((4, 4, 4, 2))]
    offset = ((away[0] * 4 + away[1]) * 4 + away[2]) * 2 + away[3]
    rank = dot(ranks[...], onehot(iota((128, 512), 0) == offset))[0:1]
    row = iota((8, 512), 0)
    pair = jnp.where(row == 0, rank, jnp.where(row == 1, ordinal, 0.0)).astype(BF)
    for o in range(2):
        chosen = onehot(iota((512, 512), 0) == target_of[o : o + 1, :])
        picked = dot(pair, chosen)
        slots[o : o + 1, :] = (picked[0:1] * SLOTS + picked[1:2]).astype(I32)
    rank = rank.astype(I32)
    to_rank = onehot(iota((128, 512), 0) == rank)
    at_lane = iota((128, 512), 0) == ordinal.astype(I32) + SLOTS * (rank % 8)
    block = block_of[...]
    upper = jnp.where(at_lane, (block // 16).astype(F32), 0.0).astype(BF)
    lower = jnp.where(at_lane, (block % 16).astype(F32), 0.0).astype(BF)
    block_rows[...] = dot_nt(to_rank, upper) * 16.0 + dot_nt(to_rank, lower)


def middle_eigen(j00, j01, j02, j10, j11, j12, j20, j21, j22):
    p01 = j01 * j10
    p02 = j02 * j20
    p12 = j12 * j21
    m00 = j00 * j00 + (p01 + p02)
    m11 = j11 * j11 + (p01 + p12)
    m22 = j22 * j22 + (p02 + p12)
    n01 = (j00 + j11) * (j01 + j10) + (j02 * j21 + j12 * j20)
    n02 = (j00 + j22) * (j02 + j20) + (j01 * j12 + j21 * j10)
    n12 = (j11 + j22) * (j12 + j21) + (j10 * j02 + j20 * j01)
    q = (m00 + m11 + m22) * (1.0 / 3.0)
    a00 = m00 - q
    a11 = m11 - q
    a22 = m22 - q
    s01 = n01 * n01
    s02 = n02 * n02
    s12 = n12 * n12
    a00x2 = a00 + a00
    minor = 4.0 * a11 * a22
    s_12 = (a00x2 * a00x2 - minor) + (s01 + s02 + s12)
    det_4 = a00 * (minor - s12) - (a11 * s02 + a22 * s01) + n01 * n02 * n12
    s_12 = jnp.maximum(s_12, 1e-24)
    inverse = lax.rsqrt(s_12)
    ratio = (det_4 * (3.0 * math.sqrt(3.0))) * (inverse * inverse * inverse)
    rest = jnp.maximum(1.0 - ratio * ratio, 1e-30)
    cosine = rest * lax.rsqrt(rest)
    poly = THIRD_POLY[-1]
    for coefficient in THIRD_POLY[-2::-1]:
        poly = poly * cosine + coefficient
    return q - (s_12 * inverse) * (ratio * poly)


def stitch_y(first, last):
    normal = iota((8, CROSS), 1) // EZN
    return (
        jnp.where(normal > 0, 0.5 * (first + pltpu.roll(last, EZN, 1)), first),
        jnp.where(normal < EYN - 1, 0.5 * (last + pltpu.roll(first, CROSS - EZN, 1)), last),
    )


def stitch_z(first, last):
    lane = iota((8, CROSS), 1)
    span = lane % EZN
    row = lane - span

    def picked(values, step):
        at = row + (span + step) % EZN
        return jnp.take_along_axis(values, at, axis=1, mode="promise_in_bounds")

    before = picked(last, EZN - 1)
    after = picked(first, 1)
    return 0.5 * (first + before), 0.5 * (last + after)


def stitch_plane(grad, layer, firsts, lasts, stitch):
    pairs = [(grad[layer, m, firsts, :], grad[layer, m, lasts, :]) for m in range(9)]
    pairs = [stitch(first, last) for first, last in pairs]
    for m in range(9):
        grad[layer, m, firsts, :] = pairs[m][0]
        grad[layer, m, lasts, :] = pairs[m][1]


def stitch_plane_z(grad, layer, base):
    stitch_plane(grad, layer, pl.ds(base, 8, stride=8), pl.ds(base + 7, 8, stride=8), stitch_z)


def eigen_plane(grad, lam, layer, base):
    for j in range(8):
        at = pl.ds(base + 8 * j, 8)
        lam[layer, at, :] = middle_eigen(*[grad[layer, m, at, :] for m in range(9)])


def resample(layer, o, lam, res_x, res_y, res_z, rows, stage_z, stage_y):
    lanes = pl.ds(pl.multiple_of(layer * CROSS, CROSS), CROSS)

    def along_z(i, carry):
        base = i * 64
        points = [lam[layer, pl.ds(base + k, 8, stride=8), :] for k in range(8)]
        for w in range(4):
            total = points[0] * res_z[o, w, 0:1, lanes]
            for k in range(1, 8):
                total = total + points[k] * res_z[o, w, k : k + 1, lanes]
            stage_z[pl.ds(pl.multiple_of(w * 64 + i * 8, 8), 8), :] = total
        return carry

    lax.fori_loop(0, 8, along_z, 0, unroll=8)
    for w in range(4):
        points = [stage_z[pl.ds(w * 64 + j, 8, stride=8), :] for j in range(8)]
        for v in range(4):
            total = points[0] * res_y[o, v, 0:1, lanes]
            for j in range(1, 8):
                total = total + points[j] * res_y[o, v, j : j + 1, lanes]
            stage_y[32 * v + 8 * w : 32 * v + 8 * w + 8, :] = total
    points = [
        jnp.concatenate(
            [stage_y[pl.ds(i, 8, stride=8), :], stage_y[pl.ds(64 + i, 8, stride=8), :]], axis=0
        )
        for i in range(8)
    ]
    totals = []
    for u in range(8):
        total = points[0] * res_x[o, u, 0:1, lanes]
        for i in range(1, 8):
            total = total + points[i] * res_x[o, u, i : i + 1, lanes]
        totals.append(total)
    piece = jnp.concatenate(totals, axis=0).T
    upper = piece.astype(BF)
    at = pl.ds(pl.multiple_of(o * 512 + layer * CROSS, CROSS), CROSS)
    rows[at, 0:128] = upper
    rows[at, 128:256] = (piece - upper.astype(F32)).astype(BF)


def differentiate(vel, op_x, op_yz, inv, grad, rims, vel_loads):
    for c in range(3):
        vel_loads[c].wait()
        along_x = dot(op_x[...], vel[c])
        halves = [dot(op_yz[...], vel[c, 256 * half : 256 * half + 256, :]) for half in range(2)]
        for a in range(3):
            m = 3 * c + a

            def block(i, layer, a=a):
                lanes = slice(CROSS * layer, CROSS * layer + CROSS)
                if a == 0:
                    rows = along_x[64 * i : 64 * i + 64, lanes]
                else:
                    at = 256 * (a - 1) + 64 * (i % 4)
                    rows = halves[i // 4][at : at + 64, lanes]
                return rows * inv[a : a + 1, lanes]

            rims[0, m] = block(0, 0)
            rims[1, m] = block(7, LAYERS - 1)
            for layer in range(LAYERS):
                for i in range(1, 8):
                    if i == 7 and layer == LAYERS - 1:
                        continue
                    values = block(i, layer)
                    if i == 7:
                        values = 0.5 * (values + block(0, layer + 1))
                    first, last = stitch_y(values[0:8], values[56:64])
                    places = [(layer, 64 * i)] + ([(layer + 1, 0)] if i == 7 else [])
                    for place, base in places:
                        grad[place, m, base : base + 8, :] = first
                        grad[place, m, base + 8 : base + 56, :] = values[8:56]
                        grad[place, m, base + 56 : base + 64, :] = last


def kernel(
    inv_h, op_x_h, op_yz_h, ranks_h, target_h, brick_h, block_h, home_h, x_h, y_h, z_h, vel_h,
    bricks,
    inv, op_x, op_yz, ranks, target_of, brick_of, block_of, home_of, res_x, res_y, res_z, vel,
    rims, halo, grad, lam, stage_z, stage_y, rows, slots, block_rows, source, landed, landed_blocks, places,
    load_sems, vel_sems, halo_send, halo_recv, send_sem, recv_sems, block_send, block_recv, own_sem,
):
    me = lax.axis_index("dom")
    count = lax.axis_size("dom")
    mesh_id = pl.DeviceIdType.MESH
    y, x, z, core = torus(me)
    parts = (
        [lax.rem(y + k, 4) * 32 for k in range(4)],
        [lax.rem(x + k, 4) * 8 for k in range(4)],
        [lax.rem(z + k, 4) * 2 for k in range(4)],
        [lax.rem(core + k, 2) for k in range(2)],
    )
    peers = [sum(part[k] for part, k in zip(parts, offset)) for offset in OFFSETS[:-1]]

    far = (inv_h, op_x_h, op_yz_h, ranks_h, target_h, brick_h, block_h, home_h, x_h, y_h, z_h)
    near = (inv, op_x, op_yz, ranks, target_of, brick_of, block_of, home_of, res_x, res_y, res_z)
    loads = [pltpu.make_async_copy(f, n, load_sems.at[k]) for k, (f, n) in enumerate(zip(far, near))]
    vel_loads = [pltpu.make_async_copy(vel_h.at[c], vel.at[c], vel_sems.at[c]) for c in range(3)]
    for load in loads[:2] + vel_loads[:1] + loads[2:3] + vel_loads[1:] + loads[3:]:
        load.start()
    barrier = pltpu.get_barrier_semaphore()
    for peer in peers:
        pl.semaphore_signal(barrier, inc=1, device_id=(peer,), device_id_type=mesh_id)
    for load in loads[:3]:
        load.wait()
    differentiate(vel, op_x, op_yz, inv, grad, rims, vel_loads)

    def plane_z(t, carry):
        stitch_plane_z(grad, t // 8, pl.multiple_of(lax.rem(t, 8) * 64, 64))
        return carry

    def plane_eigen(t, carry):
        eigen_plane(grad, lam, t // 8, pl.multiple_of(lax.rem(t, 8) * 64, 64))
        return carry

    lax.fori_loop(1, 31, plane_z, 0, unroll=2)
    for load in loads[3:8]:
        load.wait()
    route(ranks, target_of, brick_of, block_of, home_of, slots, block_rows)

    pl.semaphore_wait(barrier, count - 1)
    sends = [
        pltpu.make_async_remote_copy(
            src_ref=rims.at[side], dst_ref=halo.at[1 - side],
            send_sem=halo_send.at[side], recv_sem=halo_recv.at[1 - side],
            device_id=(lax.rem(me + step, count),), device_id_type=mesh_id,
        )
        for side, step in ((0, count - 1), (1, 1))
    ]
    for send in sends:
        send.start()
    for rank, peer in enumerate(peers):
        pltpu.make_async_remote_copy(
            src_ref=block_rows.at[pl.ds(rank, 1)], dst_ref=landed_blocks.at[pl.ds(rank, 1)],
            send_sem=block_send, recv_sem=block_recv,
            device_id=(peer,), device_id_type=mesh_id,
        ).start()

    lax.fori_loop(1, 31, plane_eigen, 0, unroll=2)
    for load in loads[8:]:
        load.wait()

    def resample_of(layer_of):
        def both(n, carry):
            for o in range(2):
                resample(layer_of(n), o, lam, res_x, res_y, res_z, rows, stage_z, stage_y)
            return carry

        return both

    lax.fori_loop(0, 2, resample_of(lambda n: n + 1), 0)
    for send in sends:
        send.wait_recv()
    for side, layer, base in ((0, 0, 0), (1, LAYERS - 1, 448)):
        for m in range(9):
            grad[layer, m, base : base + 64, :] = 0.5 * (rims[side, m] + halo[side, m])
        stitch_plane(grad, layer, slice(base, base + 8), slice(base + 56, base + 64), stitch_y)
    for layer, base in ((0, 0), (LAYERS - 1, 448)):
        stitch_plane_z(grad, layer, base)
    for layer, base in ((0, 0), (LAYERS - 1, 448)):
        eigen_plane(grad, lam, layer, base)
    lax.fori_loop(0, 2, resample_of(lambda n: n * (LAYERS - 1)), 0)

    slot_row = jnp.concatenate([slots[0:1, :], slots[1:2, :]], axis=1)

    def push(chunk):
        for rank in range(16 * chunk, min(16 * chunk + 16, 127)):
            pltpu.make_async_remote_copy(
                src_ref=source.at[rank], dst_ref=landed.at[rank],
                send_sem=send_sem, recv_sem=recv_sems.at[chunk],
                device_id=(peers[rank],), device_id_type=mesh_id,
            ).start()

    pushed = 0
    for chunk, chunks in PACKS:
        at = slice(16 * chunk, 16 * chunk + 16 * chunks)
        chosen = onehot(iota((256 * chunks, 1024), 0) + chunk * 256 == slot_row)
        packed = dot(chosen, rows[...])
        source[at] = (packed[:, 0:128] + packed[:, 128:256]).reshape(16 * chunks, SLOTS, 128)
        while pushed < chunk:
            push(pushed)
            pushed += 1
    for send in sends:
        send.wait_send()
    while pushed < 8:
        push(pushed)
        pushed += 1
    own = pltpu.make_async_copy(source.at[127], landed.at[127], own_sem)
    own.start()
    own.wait()

    def drained(ref, send, recv):
        return pltpu.make_async_remote_copy(
            src_ref=ref, dst_ref=ref, send_sem=send, recv_sem=recv,
            device_id=(me,), device_id_type=mesh_id,
        )

    blocks_in = drained(landed_blocks.at[pl.ds(0, count - 1)], block_send, block_recv)
    blocks_in.wait_recv()
    blocks_in.wait_send()
    landed_blocks[127:128, :] = block_rows[127:128, :]
    named = jnp.sum(landed_blocks[...].reshape(16, 8, 128), axis=1).astype(I32)

    def place(step, carry):
        base = pl.multiple_of(step * 256, 256)
        row = iota((256, 128), 0) + base
        for n in range(16):
            places[pl.ds(base, 256), 128 * n : 128 * n + 128] = onehot(row == named[n : n + 1, :])
        return carry

    lax.fori_loop(0, 8, place, 0)

    def unpack(chunk, chunks):
        for n in range(chunk, chunk + chunks):
            part = landed.at[pl.ds(16 * n, 15 if n == 7 else 16)]
            drained(part, send_sem, recv_sems.at[n]).wait_recv()
        values = landed[16 * chunk : 16 * chunk + 16 * chunks].reshape(256 * chunks, 128)
        upper = values.astype(BF)
        lower = (values - upper.astype(F32)).astype(BF)
        both = jnp.concatenate([upper, lower], axis=1)
        for part in range(4):
            at = slice(512 * part, 512 * part + 512)
            term = dot(places[at, 256 * chunk : 256 * chunk + 256 * chunks], both)
            term = term[:, 0:128] + term[:, 128:256]
            bricks[0, at, :] = term if chunk == 0 else bricks[0, at, :] + term

    for chunk, chunks in GROUPS:
        unpack(chunk, chunks)
    drained(source.at[pl.ds(0, count - 1)], send_sem, recv_sems.at[0]).wait_send()


def operators():
    d = diff_matrix()
    one = np.eye(8)
    op_x = np.kron(np.kron(d, one), one)
    op_y = np.kron(np.kron(np.eye(4), d), one)
    op_z = np.kron(np.eye(32), d)
    return [jnp.asarray(op, F32).astype(BF) for op in (op_x, np.concatenate([op_y, op_z]))]


def shards(velocity, inverse_sizes, resample_x, resample_y, resample_z, piece_target, target_brick, target_block, brick_home):
    op_x, op_yz = operators()
    ranks = np.zeros((8, 128), np.float32)
    for rank, (y, x, z, core) in enumerate(OFFSETS):
        ranks[:, ((y * 4 + x) * 4 + z) * 2 + core] = rank
    operands = (
        inverse_sizes, op_x, op_yz, jnp.asarray(ranks).astype(BF),
        piece_target, target_brick.reshape(1, 512), target_block.reshape(1, 512), brick_home.reshape(1, 128),
        resample_x, resample_y, resample_z, velocity,
    )
    scratch = [pltpu.VMEM(array.shape, array.dtype) for array in operands]
    scratch += [
        pltpu.VMEM((2, 9, 64, 128), F32),
        pltpu.VMEM((2, 9, 64, 128), F32),
        pltpu.VMEM((LAYERS, 9, 512, 128), F32),
        pltpu.VMEM((LAYERS, 512, 128), F32),
        pltpu.VMEM((256, 128), F32),
        pltpu.VMEM((128, 128), F32),
        pltpu.VMEM((1024, 256), BF),
        pltpu.VMEM((2, 512), I32),
        pltpu.VMEM((128, 128), F32),
        pltpu.VMEM((128, SLOTS, 128), F32),
        pltpu.VMEM((128, SLOTS, 128), F32),
        pltpu.VMEM((128, 128), F32),
        pltpu.VMEM((BLOCKS, BLOCKS), BF),
        pltpu.SemaphoreType.DMA((len(operands) - 1,)),
        pltpu.SemaphoreType.DMA((3,)),
        pltpu.SemaphoreType.DMA((2,)),
        pltpu.SemaphoreType.DMA((2,)),
        pltpu.SemaphoreType.DMA,
        pltpu.SemaphoreType.DMA((8,)),
        pltpu.SemaphoreType.DMA,
        pltpu.SemaphoreType.DMA,
        pltpu.SemaphoreType.DMA,
    ]
    return pl.pallas_call(
        kernel,
        in_specs=[pl.BlockSpec(memory_space=pltpu.HBM)] * len(operands),
        out_specs=pl.BlockSpec(memory_space=pltpu.VMEM),
        out_shape=jax.ShapeDtypeStruct((1, BLOCKS, 128), F32),
        scratch_shapes=scratch,
        compiler_params=pltpu.CompilerParams(
            collective_id=0, has_side_effects=True, vmem_limit_bytes=VMEM_LIMIT
        ),
        name="step",
    )(*[pltpu.with_memory_space_constraint(operand, pltpu.HBM) for operand in operands])


def solution(mesh):
    return jax.shard_map(
        shards,
        mesh=mesh,
        in_specs=(
            P(None, None, "dom"),
            P(None, "dom"),
            P(None, None, None, "dom"),
            P(None, None, None, "dom"),
            P(None, None, None, "dom"),
            P(None, "dom"),
            P("dom", None),
            P("dom"),
            P(),
        ),
        out_specs=P("dom", None, None),
        check_vma=False,
    )
```

```python
import math

import jax
import jax.numpy as jnp
import numpy as np
from jax import lax
from jax.experimental import pallas as pl
from jax.experimental.pallas import tpu as pltpu
from jax.sharding import PartitionSpec as P

EYN = 8
EZN = 16
BLOCKS = 2048
CROSS = 128
LAYERS = 4
SLOTS = 16
FACE = 392
BF = jnp.bfloat16
F32 = jnp.float32
I32 = jnp.int32
VMEM_LIMIT = 40 << 20

GLL_NODES = [
    -1.0,
    -0.8717401485096066,
    -0.5917001814331423,
    -0.2092992179024789,
    0.2092992179024789,
    0.5917001814331423,
    0.8717401485096066,
    1.0,
]

THIRD_POLY = (
    0.28867512941360474,
    -0.16666603088378906,
    0.12827838957309723,
    -0.10773465782403946,
    0.09301131963729858,
    -0.0773678869009018,
    0.0560062974691391,
    -0.03085879236459732,
    0.010898211039602757,
    -0.0017919066594913602,
)


def far_first():
    hops = (0, 1, 2, 1)
    offsets = [np.unravel_index(n, (4, 4, 4, 2)) for n in np.random.RandomState(1).permutation(128)]
    offsets.sort(key=lambda at: (any(at) == 0, -hops[at[0]] - hops[at[1]] - hops[at[2]]))
    return [tuple(int(part) for part in at) for at in offsets]


OFFSETS = far_first()
PACKS = ((0, 2), (2, 2), (4, 2), (6, 2))
GROUPS = ((0, 2), (2, 2), (4, 2), (6, 2))


def diff_matrix():
    nodes = GLL_NODES
    weights = []
    for first in range(8):
        product_term = 1.0
        for other in range(8):
            if other != first:
                product_term = product_term * (nodes[first] - nodes[other])
        weights.append(1.0 / product_term)
    rows = []
    for first in range(8):
        row = []
        for second in range(8):
            if second == first:
                row.append(0.0)
            else:
                row.append(weights[second] / weights[first] / (nodes[first] - nodes[second]))
        row[first] = -sum(row)
        rows.append(row)
    return np.array(rows)


def iota(shape, dim):
    return lax.broadcasted_iota(I32, shape, dim)


def onehot(mask):
    return jnp.where(mask, 1.0, 0.0).astype(BF)


def dot(a, b):
    return jnp.dot(a, b, preferred_element_type=F32)


def dot_nt(a, b):
    return lax.dot_general(a, b, (((1,), (1,)), ((), ())), preferred_element_type=F32)


def torus(index):
    return index // 32, (index // 8) % 4, (index // 2) % 4, index % 2


def route(ranks, target_of, brick_of, block_of, home_of, joins, slots, block_rows):
    here = torus(lax.axis_index("dom"))
    same = iota((128, 512), 0) == brick_of[...]
    member = onehot(same)
    earlier = onehot(iota((512, 512), 0) < iota((512, 512), 1))
    ordinal = jnp.sum(jnp.where(same, dot(member, earlier), 0.0), axis=0, keepdims=True)
    homes = jnp.broadcast_to(home_of[...].astype(F32), (8, 128)).astype(BF)
    there = torus(dot(homes, member)[0:1].astype(I32))
    away = [(there[k] - here[k] + size) % size for k, size in enumerate((4, 4, 4, 2))]
    offset = ((away[0] * 4 + away[1]) * 4 + away[2]) * 2 + away[3]
    rank = dot(ranks[...], onehot(iota((128, 512), 0) == offset))[0:1]
    for o in range(2):
        joins[:, 512 * o : 512 * o + 512] = onehot(iota((512, 512), 0) == target_of[o : o + 1, :])
    rank = rank.astype(I32)
    slots[...] = rank * SLOTS + ordinal.astype(I32)
    to_rank = onehot(iota((128, 512), 0) == rank)
    at_lane = iota((128, 512), 0) == ordinal.astype(I32) + SLOTS * (rank % 8)
    block = block_of[...]
    upper = jnp.where(at_lane, (block // 16).astype(F32), 0.0).astype(BF)
    lower = jnp.where(at_lane, (block % 16).astype(F32), 0.0).astype(BF)
    block_rows[...] = dot_nt(to_rank, upper) * 16.0 + dot_nt(to_rank, lower)


def middle_eigen(j00, j01, j02, j10, j11, j12, j20, j21, j22):
    p01 = j01 * j10
    p02 = j02 * j20
    p12 = j12 * j21
    m00 = j00 * j00 + (p01 + p02)
    m11 = j11 * j11 + (p01 + p12)
    m22 = j22 * j22 + (p02 + p12)
    n01 = (j00 + j11) * (j01 + j10) + (j02 * j21 + j12 * j20)
    n02 = (j00 + j22) * (j02 + j20) + (j01 * j12 + j21 * j10)
    n12 = (j11 + j22) * (j12 + j21) + (j10 * j02 + j20 * j01)
    q = (m00 + m11 + m22) * (1.0 / 3.0)
    a00 = m00 - q
    a11 = m11 - q
    a22 = m22 - q
    s01 = n01 * n01
    s02 = n02 * n02
    s12 = n12 * n12
    a00x2 = a00 + a00
    minor = 4.0 * a11 * a22
    s_12 = (a00x2 * a00x2 - minor) + (s01 + s02 + s12)
    det_4 = a00 * (minor - s12) - (a11 * s02 + a22 * s01) + n01 * n02 * n12
    s_12 = jnp.maximum(s_12, 1e-24)
    inverse = lax.rsqrt(s_12)
    ratio = (det_4 * (3.0 * math.sqrt(3.0))) * (inverse * inverse * inverse)
    rest = jnp.maximum(1.0 - ratio * ratio, 1e-30)
    cosine = rest * lax.rsqrt(rest)
    poly = THIRD_POLY[-1]
    for coefficient in THIRD_POLY[-2::-1]:
        poly = poly * cosine + coefficient
    return q - (s_12 * inverse) * (ratio * poly)


def stitch_y(first, last):
    normal = iota((8, CROSS), 1) // EZN
    return (
        jnp.where(normal > 0, 0.5 * (first + pltpu.roll(last, EZN, 1)), first),
        jnp.where(normal < EYN - 1, 0.5 * (last + pltpu.roll(first, CROSS - EZN, 1)), last),
    )


def stitch_z(first, last):
    lane = iota((8, CROSS), 1)
    span = lane % EZN
    row = lane - span

    def picked(values, step):
        at = row + (span + step) % EZN
        return jnp.take_along_axis(values, at, axis=1, mode="promise_in_bounds")

    before = picked(last, EZN - 1)
    after = picked(first, 1)
    return 0.5 * (first + before), 0.5 * (last + after)


def stitch_plane(grad, layer, firsts, lasts, stitch):
    pairs = [(grad[layer, m, firsts, :], grad[layer, m, lasts, :]) for m in range(9)]
    pairs = [stitch(first, last) for first, last in pairs]
    for m in range(9):
        grad[layer, m, firsts, :] = pairs[m][0]
        grad[layer, m, lasts, :] = pairs[m][1]


def stitch_plane_z(grad, layer, base):
    stitch_plane(grad, layer, pl.ds(base, 8, stride=8), pl.ds(base + 7, 8, stride=8), stitch_z)


def eigen_plane(grad, lam, layer, base):
    for j in range(8):
        at = pl.ds(base + 8 * j, 8)
        lam[layer, at, :] = middle_eigen(*[grad[layer, m, at, :] for m in range(9)])


def resample(layer, o, lam, res_x, res_y, res_z, rows, stage_z, stage_y):
    lanes = pl.ds(pl.multiple_of(layer * CROSS, CROSS), CROSS)

    def along_z(i, carry):
        base = i * 64
        points = [lam[layer, pl.ds(base + k, 8, stride=8), :] for k in range(8)]
        for w in range(4):
            total = points[0] * res_z[o, w, 0:1, lanes]
            for k in range(1, 8):
                total = total + points[k] * res_z[o, w, k : k + 1, lanes]
            stage_z[pl.ds(pl.multiple_of(w * 64 + i * 8, 8), 8), :] = total
        return carry

    lax.fori_loop(0, 8, along_z, 0, unroll=8)
    for w in range(4):
        points = [stage_z[pl.ds(w * 64 + j, 8, stride=8), :] for j in range(8)]
        for v in range(4):
            total = points[0] * res_y[o, v, 0:1, lanes]
            for j in range(1, 8):
                total = total + points[j] * res_y[o, v, j : j + 1, lanes]
            stage_y[32 * v + 8 * w : 32 * v + 8 * w + 8, :] = total
    points = [
        jnp.concatenate(
            [stage_y[pl.ds(i, 8, stride=8), :], stage_y[pl.ds(64 + i, 8, stride=8), :]], axis=0
        )
        for i in range(8)
    ]
    totals = []
    for u in range(8):
        total = points[0] * res_x[o, u, 0:1, lanes]
        for i in range(1, 8):
            total = total + points[i] * res_x[o, u, i : i + 1, lanes]
        totals.append(total)
    piece = jnp.concatenate(totals, axis=0).T
    upper = piece.astype(BF)
    at = pl.ds(pl.multiple_of(o * 512 + layer * CROSS, CROSS), CROSS)
    rows[at, 0:128] = upper
    rows[at, 128:256] = (piece - upper.astype(F32)).astype(BF)


def differentiate(vel, op_x, op_yz, inv, grad, rims, faces, vel_loads):
    for c in range(3):
        vel_loads[c].wait()
        along_x = dot(op_x[...], vel[c])
        halves = [dot(op_yz[...], vel[c, 256 * half : 256 * half + 256, :]) for half in range(2)]
        for a in range(3):
            m = 3 * c + a

            def block(i, layer, a=a):
                lanes = slice(CROSS * layer, CROSS * layer + CROSS)
                if a == 0:
                    rows = along_x[64 * i : 64 * i + 64, lanes]
                else:
                    at = 256 * (a - 1) + 64 * (i % 4)
                    rows = halves[i // 4][at : at + 64, lanes]
                return rows * inv[a : a + 1, lanes]

            for side, i, layer in ((0, 0, 0), (1, 7, LAYERS - 1)):
                values = block(i, layer)
                rims[side, m] = values
                if a == 0:
                    lanes = slice(CROSS * layer, CROSS * layer + CROSS)
                    points = vel[c, 64 * i : 64 * i + 64, lanes]
                    faces[side, 64 * c : 64 * c + 64, :] = values
                    faces[side, 192 + 64 * c : 256 + 64 * c, :] = points.astype(F32)
                    if c == 0:
                        faces[side, 384:FACE, :] = jnp.zeros((8, CROSS), F32)
                        faces[side, 384:387, :] = inv[:, lanes]
            for layer in range(LAYERS):
                for i in range(1, 8):
                    if i == 7 and layer == LAYERS - 1:
                        continue
                    values = block(i, layer)
                    if i == 7:
                        values = 0.5 * (values + block(0, layer + 1))
                    first, last = stitch_y(values[0:8], values[56:64])
                    places = [(layer, 64 * i)] + ([(layer + 1, 0)] if i == 7 else [])
                    for place, base in places:
                        grad[place, m, base : base + 8, :] = first
                        grad[place, m, base + 8 : base + 56, :] = values[8:56]
                        grad[place, m, base + 56 : base + 64, :] = last


def kernel(
    inv_h, op_x_h, op_yz_h, ranks_h, target_h, brick_h, block_h, home_h, x_h, y_h, z_h, vel_h,
    bricks,
    inv, op_x, op_yz, ranks, target_of, brick_of, block_of, home_of, res_x, res_y, res_z, vel,
    rims, faces, halo, grad, lam, stage_z, stage_y, rows, joins, slots, sums, block_rows, source, landed, landed_blocks, places,
    load_sems, vel_sems, halo_send, halo_recv, send_sem, recv_sems, block_send, block_recv, own_sem,
):
    me = lax.axis_index("dom")
    count = lax.axis_size("dom")
    mesh_id = pl.DeviceIdType.MESH
    y, x, z, core = torus(me)
    parts = (
        [lax.rem(y + k, 4) * 32 for k in range(4)],
        [lax.rem(x + k, 4) * 8 for k in range(4)],
        [lax.rem(z + k, 4) * 2 for k in range(4)],
        [lax.rem(core + k, 2) for k in range(2)],
    )
    peers = [sum(part[k] for part, k in zip(parts, offset)) for offset in OFFSETS[:-1]]

    far = (inv_h, op_x_h, op_yz_h, ranks_h, target_h, brick_h, block_h, home_h, x_h, y_h, z_h)
    near = (inv, op_x, op_yz, ranks, target_of, brick_of, block_of, home_of, res_x, res_y, res_z)
    loads = [pltpu.make_async_copy(f, n, load_sems.at[k]) for k, (f, n) in enumerate(zip(far, near))]
    vel_loads = [pltpu.make_async_copy(vel_h.at[c], vel.at[c], vel_sems.at[c]) for c in range(3)]
    for load in loads[:2] + vel_loads[:1] + loads[2:3] + vel_loads[1:] + loads[3:]:
        load.start()
    barrier = pltpu.get_barrier_semaphore()
    for peer in peers:
        pl.semaphore_signal(barrier, inc=1, device_id=(peer,), device_id_type=mesh_id)
    for load in loads[:3]:
        load.wait()
    differentiate(vel, op_x, op_yz, inv, grad, rims, faces, vel_loads)

    def plane_z(t, carry):
        stitch_plane_z(grad, t // 8, pl.multiple_of(lax.rem(t, 8) * 64, 64))
        return carry

    def plane_eigen(t, carry):
        eigen_plane(grad, lam, t // 8, pl.multiple_of(lax.rem(t, 8) * 64, 64))
        return carry

    lax.fori_loop(1, 31, plane_z, 0, unroll=2)
    pl.semaphore_wait(barrier, count - 1)
    sends = [
        pltpu.make_async_remote_copy(
            src_ref=faces.at[side], dst_ref=halo.at[1 - side],
            send_sem=halo_send.at[side], recv_sem=halo_recv.at[1 - side],
            device_id=(lax.rem(me + step, count),), device_id_type=mesh_id,
        )
        for side, step in ((0, count - 1), (1, 1))
    ]
    for send in sends:
        send.start()
    lax.fori_loop(1, 31, plane_eigen, 0, unroll=5)
    for load in loads[3:8]:
        load.wait()
    route(ranks, target_of, brick_of, block_of, home_of, joins, slots, block_rows)

    for rank, peer in enumerate(peers):
        pltpu.make_async_remote_copy(
            src_ref=block_rows.at[pl.ds(rank, 1)], dst_ref=landed_blocks.at[pl.ds(rank, 1)],
            send_sem=block_send, recv_sem=block_recv,
            device_id=(peer,), device_id_type=mesh_id,
        ).start()

    for load in loads[8:]:
        load.wait()

    def resample_of(layer_of):
        def both(n, carry):
            for o in range(2):
                resample(layer_of(n), o, lam, res_x, res_y, res_z, rows, stage_z, stage_y)
            return carry

        return both

    lax.fori_loop(0, 2, resample_of(lambda n: n + 1), 0)
    for send in sends:
        send.wait_recv()
    for side, layer, base in ((0, 0, 0), (1, LAYERS - 1, 448)):
        points = jnp.concatenate([halo[side, 192 + 64 * c : 256 + 64 * c, :] for c in range(3)], axis=1)
        along_face = dot(
            jnp.concatenate([op_yz[0:64, 0:64], op_yz[256:320, 0:64]], axis=0), points.astype(BF)
        )
        for c in range(3):
            for a in range(3):
                m = 3 * c + a
                if a == 0:
                    other = halo[side, 64 * c : 64 * c + 64, :]
                else:
                    other = along_face[64 * a - 64 : 64 * a, CROSS * c : CROSS * c + CROSS]
                    other = other * halo[side, 384 + a : 385 + a, :]
                grad[layer, m, base : base + 64, :] = 0.5 * (rims[side, m] + other)
        stitch_plane(grad, layer, slice(base, base + 8), slice(base + 56, base + 64), stitch_y)
    for layer, base in ((0, 0), (LAYERS - 1, 448)):
        stitch_plane_z(grad, layer, base)
    for layer, base in ((0, 0), (LAYERS - 1, 448)):
        eigen_plane(grad, lam, layer, base)
    lax.fori_loop(0, 2, resample_of(lambda n: n * (LAYERS - 1)), 0)

    for part in range(2):
        at = slice(256 * part, 256 * part + 256)
        total = dot(joins[at, :], rows[...])
        total = total[:, 0:128] + total[:, 128:256]
        upper = total.astype(BF)
        sums[at, 0:128] = upper
        sums[at, 128:256] = (total - upper.astype(F32)).astype(BF)

    def push(chunk):
        for rank in range(16 * chunk, min(16 * chunk + 16, 127)):
            pltpu.make_async_remote_copy(
                src_ref=source.at[rank], dst_ref=landed.at[rank],
                send_sem=send_sem, recv_sem=recv_sems.at[chunk],
                device_id=(peers[rank],), device_id_type=mesh_id,
            ).start()

    pushed = 0
    for chunk, chunks in PACKS:
        at = slice(16 * chunk, 16 * chunk + 16 * chunks)
        chosen = onehot(iota((256 * chunks, 512), 0) + chunk * 256 == slots[...])
        packed = dot(chosen, sums[...])
        source[at] = (packed[:, 0:128] + packed[:, 128:256]).reshape(16 * chunks, SLOTS, 128)
        while pushed < chunk:
            push(pushed)
            pushed += 1
    for send in sends:
        send.wait_send()
    while pushed < 8:
        push(pushed)
        pushed += 1
    own = pltpu.make_async_copy(source.at[127], landed.at[127], own_sem)
    own.start()
    own.wait()

    def drained(ref, send, recv):
        return pltpu.make_async_remote_copy(
            src_ref=ref, dst_ref=ref, send_sem=send, recv_sem=recv,
            device_id=(me,), device_id_type=mesh_id,
        )

    blocks_in = drained(landed_blocks.at[pl.ds(0, count - 1)], block_send, block_recv)
    blocks_in.wait_recv()
    blocks_in.wait_send()
    landed_blocks[127:128, :] = block_rows[127:128, :]
    named = jnp.sum(landed_blocks[...].reshape(16, 8, 128), axis=1).astype(I32)

    def place(step, carry):
        base = pl.multiple_of(step * 256, 256)
        row = iota((256, 128), 0) + base
        for n in range(16):
            places[pl.ds(base, 256), 128 * n : 128 * n + 128] = onehot(row == named[n : n + 1, :])
        return carry

    lax.fori_loop(0, 8, place, 0)

    def unpack(chunk, chunks):
        for n in range(chunk, chunk + chunks):
            part = landed.at[pl.ds(16 * n, 15 if n == 7 else 16)]
            drained(part, send_sem, recv_sems.at[n]).wait_recv()
        values = landed[16 * chunk : 16 * chunk + 16 * chunks].reshape(256 * chunks, 128)
        upper = values.astype(BF)
        lower = (values - upper.astype(F32)).astype(BF)
        both = jnp.concatenate([upper, lower], axis=1)
        for part in range(4):
            at = slice(512 * part, 512 * part + 512)
            term = dot(places[at, 256 * chunk : 256 * chunk + 256 * chunks], both)
            term = term[:, 0:128] + term[:, 128:256]
            bricks[0, at, :] = term if chunk == 0 else bricks[0, at, :] + term

    for chunk, chunks in GROUPS:
        unpack(chunk, chunks)
    drained(source.at[pl.ds(0, count - 1)], send_sem, recv_sems.at[0]).wait_send()


def operators():
    d = diff_matrix()
    one = np.eye(8)
    op_x = np.kron(np.kron(d, one), one)
    op_y = np.kron(np.kron(np.eye(4), d), one)
    op_z = np.kron(np.eye(32), d)
    return [jnp.asarray(op, F32).astype(BF) for op in (op_x, np.concatenate([op_y, op_z]))]


def shards(velocity, inverse_sizes, resample_x, resample_y, resample_z, piece_target, target_brick, target_block, brick_home):
    op_x, op_yz = operators()
    ranks = np.zeros((8, 128), np.float32)
    for rank, (y, x, z, core) in enumerate(OFFSETS):
        ranks[:, ((y * 4 + x) * 4 + z) * 2 + core] = rank
    operands = (
        inverse_sizes, op_x, op_yz, jnp.asarray(ranks).astype(BF),
        piece_target, target_brick.reshape(1, 512), target_block.reshape(1, 512), brick_home.reshape(1, 128),
        resample_x, resample_y, resample_z, velocity,
    )
    scratch = [pltpu.VMEM(array.shape, array.dtype) for array in operands]
    scratch += [
        pltpu.VMEM((2, 9, 64, 128), F32),
        pltpu.VMEM((2, FACE, 128), F32),
        pltpu.VMEM((2, FACE, 128), F32),
        pltpu.VMEM((LAYERS, 9, 512, 128), F32),
        pltpu.VMEM((LAYERS, 512, 128), F32),
        pltpu.VMEM((256, 128), F32),
        pltpu.VMEM((128, 128), F32),
        pltpu.VMEM((1024, 256), BF),
        pltpu.VMEM((512, 1024), BF),
        pltpu.VMEM((1, 512), I32),
        pltpu.VMEM((512, 256), BF),
        pltpu.VMEM((128, 128), F32),
        pltpu.VMEM((128, SLOTS, 128), F32),
        pltpu.VMEM((128, SLOTS, 128), F32),
        pltpu.VMEM((128, 128), F32),
        pltpu.VMEM((BLOCKS, BLOCKS), BF),
        pltpu.SemaphoreType.DMA((len(operands) - 1,)),
        pltpu.SemaphoreType.DMA((3,)),
        pltpu.SemaphoreType.DMA((2,)),
        pltpu.SemaphoreType.DMA((2,)),
        pltpu.SemaphoreType.DMA,
        pltpu.SemaphoreType.DMA((8,)),
        pltpu.SemaphoreType.DMA,
        pltpu.SemaphoreType.DMA,
        pltpu.SemaphoreType.DMA,
    ]
    return pl.pallas_call(
        kernel,
        in_specs=[pl.BlockSpec(memory_space=pltpu.HBM)] * len(operands),
        out_specs=pl.BlockSpec(memory_space=pltpu.VMEM),
        out_shape=jax.ShapeDtypeStruct((1, BLOCKS, 128), F32),
        scratch_shapes=scratch,
        compiler_params=pltpu.CompilerParams(
            collective_id=0, has_side_effects=True, vmem_limit_bytes=VMEM_LIMIT
        ),
        name="step",
    )(*[pltpu.with_memory_space_constraint(operand, pltpu.HBM) for operand in operands])


def solution(mesh):
    return jax.shard_map(
        shards,
        mesh=mesh,
        in_specs=(
            P(None, None, "dom"),
            P(None, "dom"),
            P(None, None, None, "dom"),
            P(None, None, None, "dom"),
            P(None, None, None, "dom"),
            P(None, "dom"),
            P("dom", None),
            P("dom"),
            P(),
        ),
        out_specs=P("dom", None, None),
        check_vma=False,
    )
```

```python
import math

import jax
import jax.numpy as jnp
import numpy as np
from jax import lax
from jax.experimental import pallas as pl
from jax.experimental.pallas import tpu as pltpu
from jax.sharding import PartitionSpec as P

EYN = 8
EZN = 16
BLOCKS = 2048
CROSS = 128
LAYERS = 4
SLOTS = 16
FACE = 392
BF = jnp.bfloat16
F32 = jnp.float32
I32 = jnp.int32
VMEM_LIMIT = 40 << 20

GLL_NODES = [
    -1.0,
    -0.8717401485096066,
    -0.5917001814331423,
    -0.2092992179024789,
    0.2092992179024789,
    0.5917001814331423,
    0.8717401485096066,
    1.0,
]

THIRD_POLY = (
    0.28867512941360474,
    -0.16666603088378906,
    0.12827838957309723,
    -0.10773465782403946,
    0.09301131963729858,
    -0.0773678869009018,
    0.0560062974691391,
    -0.03085879236459732,
    0.010898211039602757,
    -0.0017919066594913602,
)


def far_first():
    hops = (0, 1, 2, 1)
    offsets = [np.unravel_index(n, (4, 4, 4, 2)) for n in np.random.RandomState(1).permutation(128)]
    offsets.sort(key=lambda at: (any(at) == 0, -hops[at[0]] - hops[at[1]] - hops[at[2]]))
    return [tuple(int(part) for part in at) for at in offsets]


OFFSETS = far_first()
PACKS = ((0, 2), (2, 2), (4, 2), (6, 2))
GROUPS = ((0, 2), (2, 2), (4, 2), (6, 2))


def diff_matrix():
    nodes = GLL_NODES
    weights = []
    for first in range(8):
        product_term = 1.0
        for other in range(8):
            if other != first:
                product_term = product_term * (nodes[first] - nodes[other])
        weights.append(1.0 / product_term)
    rows = []
    for first in range(8):
        row = []
        for second in range(8):
            if second == first:
                row.append(0.0)
            else:
                row.append(weights[second] / weights[first] / (nodes[first] - nodes[second]))
        row[first] = -sum(row)
        rows.append(row)
    return np.array(rows)


def iota(shape, dim):
    return lax.broadcasted_iota(I32, shape, dim)


def onehot(mask):
    return jnp.where(mask, 1.0, 0.0).astype(BF)


def dot(a, b):
    return jnp.dot(a, b, preferred_element_type=F32)


def dot_nt(a, b):
    return lax.dot_general(a, b, (((1,), (1,)), ((), ())), preferred_element_type=F32)


def torus(index):
    return index // 32, (index // 8) % 4, (index // 2) % 4, index % 2


def route(ranks, target_of, brick_of, block_of, home_of, joins, slots, block_rows):
    here = torus(lax.axis_index("dom"))
    same = iota((128, 512), 0) == brick_of[...]
    member = onehot(same)
    earlier = onehot(iota((512, 512), 0) < iota((512, 512), 1))
    ordinal = jnp.sum(jnp.where(same, dot(member, earlier), 0.0), axis=0, keepdims=True)
    homes = jnp.broadcast_to(home_of[...].astype(F32), (8, 128)).astype(BF)
    there = torus(dot(homes, member)[0:1].astype(I32))
    away = [(there[k] - here[k] + size) % size for k, size in enumerate((4, 4, 4, 2))]
    offset = ((away[0] * 4 + away[1]) * 4 + away[2]) * 2 + away[3]
    rank = dot(ranks[...], onehot(iota((128, 512), 0) == offset))[0:1]
    for o in range(2):
        joins[:, 512 * o : 512 * o + 512] = onehot(iota((512, 512), 0) == target_of[o : o + 1, :])
    rank = rank.astype(I32)
    slots[...] = rank * SLOTS + ordinal.astype(I32)
    to_rank = onehot(iota((128, 512), 0) == rank)
    at_lane = iota((128, 512), 0) == ordinal.astype(I32) + SLOTS * (rank % 8)
    block = block_of[...]
    upper = jnp.where(at_lane, (block // 16).astype(F32), 0.0).astype(BF)
    lower = jnp.where(at_lane, (block % 16).astype(F32), 0.0).astype(BF)
    block_rows[...] = dot_nt(to_rank, upper) * 16.0 + dot_nt(to_rank, lower)


def middle_eigen(j00, j01, j02, j10, j11, j12, j20, j21, j22):
    p01 = j01 * j10
    p02 = j02 * j20
    p12 = j12 * j21
    m00 = j00 * j00 + (p01 + p02)
    m11 = j11 * j11 + (p01 + p12)
    m22 = j22 * j22 + (p02 + p12)
    n01 = (j00 + j11) * (j01 + j10) + (j02 * j21 + j12 * j20)
    n02 = (j00 + j22) * (j02 + j20) + (j01 * j12 + j21 * j10)
    n12 = (j11 + j22) * (j12 + j21) + (j10 * j02 + j20 * j01)
    q = (m00 + m11 + m22) * (1.0 / 3.0)
    a00 = m00 - q
    a11 = m11 - q
    a22 = m22 - q
    s01 = n01 * n01
    s02 = n02 * n02
    s12 = n12 * n12
    a00x2 = a00 + a00
    minor = 4.0 * a11 * a22
    s_12 = (a00x2 * a00x2 - minor) + (s01 + s02 + s12)
    det_4 = a00 * (minor - s12) - (a11 * s02 + a22 * s01) + n01 * n02 * n12
    s_12 = jnp.maximum(s_12, 1e-24)
    inverse = lax.rsqrt(s_12)
    ratio = (det_4 * (3.0 * math.sqrt(3.0))) * (inverse * inverse * inverse)
    rest = jnp.maximum(1.0 - ratio * ratio, 1e-30)
    cosine = rest * lax.rsqrt(rest)
    poly = THIRD_POLY[-1]
    for coefficient in THIRD_POLY[-2::-1]:
        poly = poly * cosine + coefficient
    return q - (s_12 * inverse) * (ratio * poly)


def stitch_y(first, last):
    normal = iota((8, CROSS), 1) // EZN
    return (
        jnp.where(normal > 0, 0.5 * (first + pltpu.roll(last, EZN, 1)), first),
        jnp.where(normal < EYN - 1, 0.5 * (last + pltpu.roll(first, CROSS - EZN, 1)), last),
    )


def stitch_z(first, last):
    lane = iota((8, CROSS), 1)
    span = lane % EZN
    row = lane - span

    def picked(values, step):
        at = row + (span + step) % EZN
        return jnp.take_along_axis(values, at, axis=1, mode="promise_in_bounds")

    before = picked(last, EZN - 1)
    after = picked(first, 1)
    return 0.5 * (first + before), 0.5 * (last + after)


def stitch_plane(grad, layer, firsts, lasts, stitch):
    pairs = [(grad[layer, m, firsts, :], grad[layer, m, lasts, :]) for m in range(9)]
    pairs = [stitch(first, last) for first, last in pairs]
    for m in range(9):
        grad[layer, m, firsts, :] = pairs[m][0]
        grad[layer, m, lasts, :] = pairs[m][1]


def stitch_plane_z(grad, layer, base):
    stitch_plane(grad, layer, pl.ds(base, 8, stride=8), pl.ds(base + 7, 8, stride=8), stitch_z)


def eigen_plane(grad, lam, layer, base):
    for j in range(8):
        at = pl.ds(base + 8 * j, 8)
        lam[layer, at, :] = middle_eigen(*[grad[layer, m, at, :] for m in range(9)])


def resample_along_z(layer, lam, res_z, stage_z):
    lanes = pl.ds(pl.multiple_of(layer * CROSS, CROSS), CROSS)
    for i in range(8):
        points = [lam[layer, pl.ds(64 * i + k, 8, stride=8), :] for k in range(8)]
        for o in range(2):
            for w in range(4):
                total = points[0] * res_z[o, w, 0:1, lanes]
                for k in range(1, 8):
                    total = total + points[k] * res_z[o, w, k : k + 1, lanes]
                at = 256 * o + 64 * w + 8 * i
                stage_z[at : at + 8, :] = total


def resample(layer, o, res_x, res_y, rows, stage_z, stage_y):
    lanes = pl.ds(pl.multiple_of(layer * CROSS, CROSS), CROSS)

    for w in range(4):
        points = [stage_z[pl.ds(256 * o + 64 * w + j, 8, stride=8), :] for j in range(8)]
        for v in range(4):
            total = points[0] * res_y[o, v, 0:1, lanes]
            for j in range(1, 8):
                total = total + points[j] * res_y[o, v, j : j + 1, lanes]
            stage_y[32 * v + 8 * w : 32 * v + 8 * w + 8, :] = total
    points = [
        jnp.concatenate(
            [stage_y[pl.ds(i, 8, stride=8), :], stage_y[pl.ds(64 + i, 8, stride=8), :]], axis=0
        )
        for i in range(8)
    ]
    totals = []
    for u in range(8):
        total = points[0] * res_x[o, u, 0:1, lanes]
        for i in range(1, 8):
            total = total + points[i] * res_x[o, u, i : i + 1, lanes]
        totals.append(total)
    piece = jnp.concatenate(totals, axis=0).T
    upper = piece.astype(BF)
    at = pl.ds(pl.multiple_of(o * 512 + layer * CROSS, CROSS), CROSS)
    rows[at, 0:128] = upper
    rows[at, 128:256] = (piece - upper.astype(F32)).astype(BF)


def differentiate(vel, op_x, op_yz, inv, grad, rims, faces, vel_loads):
    for c in range(3):
        vel_loads[c].wait()
        along_x = dot(op_x[...], vel[c])
        halves = [dot(op_yz[...], vel[c, 256 * half : 256 * half + 256, :]) for half in range(2)]
        for a in range(3):
            m = 3 * c + a

            def block(i, layer, a=a):
                lanes = slice(CROSS * layer, CROSS * layer + CROSS)
                if a == 0:
                    rows = along_x[64 * i : 64 * i + 64, lanes]
                else:
                    at = 256 * (a - 1) + 64 * (i % 4)
                    rows = halves[i // 4][at : at + 64, lanes]
                return rows * inv[a : a + 1, lanes]

            for side, i, layer in ((0, 0, 0), (1, 7, LAYERS - 1)):
                values = block(i, layer)
                rims[side, m] = values
                if a == 0:
                    lanes = slice(CROSS * layer, CROSS * layer + CROSS)
                    points = vel[c, 64 * i : 64 * i + 64, lanes]
                    faces[side, 64 * c : 64 * c + 64, :] = values
                    faces[side, 192 + 64 * c : 256 + 64 * c, :] = points.astype(F32)
                    if c == 0:
                        faces[side, 384:FACE, :] = jnp.zeros((8, CROSS), F32)
                        faces[side, 384:387, :] = inv[:, lanes]
            for layer in range(LAYERS):
                for i in range(1, 8):
                    if i == 7 and layer == LAYERS - 1:
                        continue
                    values = block(i, layer)
                    if i == 7:
                        values = 0.5 * (values + block(0, layer + 1))
                    first, last = stitch_y(values[0:8], values[56:64])
                    places = [(layer, 64 * i)] + ([(layer + 1, 0)] if i == 7 else [])
                    for place, base in places:
                        grad[place, m, base : base + 8, :] = first
                        grad[place, m, base + 8 : base + 56, :] = values[8:56]
                        grad[place, m, base + 56 : base + 64, :] = last


def kernel(
    inv_h, op_x_h, op_yz_h, ranks_h, target_h, brick_h, block_h, home_h, x_h, y_h, z_h, vel_h,
    bricks,
    inv, op_x, op_yz, ranks, target_of, brick_of, block_of, home_of, res_x, res_y, res_z, vel,
    rims, faces, halo, grad, lam, stage_z, stage_y, rows, joins, slots, sums, block_rows, source, landed, landed_blocks, places,
    load_sems, vel_sems, halo_send, halo_recv, send_sem, recv_sems, block_send, block_recv, own_sem,
):
    me = lax.axis_index("dom")
    count = lax.axis_size("dom")
    mesh_id = pl.DeviceIdType.MESH
    y, x, z, core = torus(me)
    parts = (
        [lax.rem(y + k, 4) * 32 for k in range(4)],
        [lax.rem(x + k, 4) * 8 for k in range(4)],
        [lax.rem(z + k, 4) * 2 for k in range(4)],
        [lax.rem(core + k, 2) for k in range(2)],
    )
    peers = [sum(part[k] for part, k in zip(parts, offset)) for offset in OFFSETS[:-1]]

    far = (inv_h, op_x_h, op_yz_h, ranks_h, target_h, brick_h, block_h, home_h, x_h, y_h, z_h)
    near = (inv, op_x, op_yz, ranks, target_of, brick_of, block_of, home_of, res_x, res_y, res_z)
    loads = [pltpu.make_async_copy(f, n, load_sems.at[k]) for k, (f, n) in enumerate(zip(far, near))]
    vel_loads = [pltpu.make_async_copy(vel_h.at[c], vel.at[c], vel_sems.at[c]) for c in range(3)]
    for load in loads[:2] + vel_loads[:1] + loads[2:3] + vel_loads[1:] + loads[3:]:
        load.start()
    barrier = pltpu.get_barrier_semaphore()
    for peer in peers:
        pl.semaphore_signal(barrier, inc=1, device_id=(peer,), device_id_type=mesh_id)
    for load in loads[:3]:
        load.wait()
    differentiate(vel, op_x, op_yz, inv, grad, rims, faces, vel_loads)

    def plane_z(t, carry):
        stitch_plane_z(grad, t // 8, pl.multiple_of(lax.rem(t, 8) * 64, 64))
        return carry

    def plane_eigen(t, carry):
        eigen_plane(grad, lam, t // 8, pl.multiple_of(lax.rem(t, 8) * 64, 64))
        return carry

    lax.fori_loop(1, 31, plane_z, 0, unroll=5)
    pl.semaphore_wait(barrier, count - 1)
    sends = [
        pltpu.make_async_remote_copy(
            src_ref=faces.at[side], dst_ref=halo.at[1 - side],
            send_sem=halo_send.at[side], recv_sem=halo_recv.at[1 - side],
            device_id=(lax.rem(me + step, count),), device_id_type=mesh_id,
        )
        for side, step in ((0, count - 1), (1, 1))
    ]
    for send in sends:
        send.start()
    lax.fori_loop(1, 31, plane_eigen, 0, unroll=5)
    for load in loads[3:8]:
        load.wait()
    route(ranks, target_of, brick_of, block_of, home_of, joins, slots, block_rows)

    for rank, peer in enumerate(peers):
        pltpu.make_async_remote_copy(
            src_ref=block_rows.at[pl.ds(rank, 1)], dst_ref=landed_blocks.at[pl.ds(rank, 1)],
            send_sem=block_send, recv_sem=block_recv,
            device_id=(peer,), device_id_type=mesh_id,
        ).start()

    for load in loads[8:]:
        load.wait()

    def resample_of(layer_of):
        def both(n, carry):
            resample_along_z(layer_of(n), lam, res_z, stage_z)
            for o in range(2):
                resample(layer_of(n), o, res_x, res_y, rows, stage_z, stage_y)
            return carry

        return both

    lax.fori_loop(0, 2, resample_of(lambda n: n + 1), 0)
    for send in sends:
        send.wait_recv()
    for side, layer, base in ((0, 0, 0), (1, LAYERS - 1, 448)):
        points = jnp.concatenate([halo[side, 192 + 64 * c : 256 + 64 * c, :] for c in range(3)], axis=1)
        along_face = dot(
            jnp.concatenate([op_yz[0:64, 0:64], op_yz[256:320, 0:64]], axis=0), points.astype(BF)
        )
        for c in range(3):
            for a in range(3):
                m = 3 * c + a
                if a == 0:
                    other = halo[side, 64 * c : 64 * c + 64, :]
                else:
                    other = along_face[64 * a - 64 : 64 * a, CROSS * c : CROSS * c + CROSS]
                    other = other * halo[side, 384 + a : 385 + a, :]
                grad[layer, m, base : base + 64, :] = 0.5 * (rims[side, m] + other)
        stitch_plane(grad, layer, slice(base, base + 8), slice(base + 56, base + 64), stitch_y)
    for layer, base in ((0, 0), (LAYERS - 1, 448)):
        stitch_plane_z(grad, layer, base)
    for layer, base in ((0, 0), (LAYERS - 1, 448)):
        eigen_plane(grad, lam, layer, base)
    lax.fori_loop(0, 2, resample_of(lambda n: n * (LAYERS - 1)), 0)

    for part in range(2):
        at = slice(256 * part, 256 * part + 256)
        total = dot(joins[at, :], rows[...])
        total = total[:, 0:128] + total[:, 128:256]
        upper = total.astype(BF)
        sums[at, 0:128] = upper
        sums[at, 128:256] = (total - upper.astype(F32)).astype(BF)

    def push(chunk):
        for rank in range(16 * chunk, min(16 * chunk + 16, 127)):
            pltpu.make_async_remote_copy(
                src_ref=source.at[rank], dst_ref=landed.at[rank],
                send_sem=send_sem, recv_sem=recv_sems.at[chunk],
                device_id=(peers[rank],), device_id_type=mesh_id,
            ).start()

    pushed = 0
    for chunk, chunks in PACKS:
        at = slice(16 * chunk, 16 * chunk + 16 * chunks)
        chosen = onehot(iota((256 * chunks, 512), 0) + chunk * 256 == slots[...])
        packed = dot(chosen, sums[...])
        source[at] = (packed[:, 0:128] + packed[:, 128:256]).reshape(16 * chunks, SLOTS, 128)
        while pushed < chunk:
            push(pushed)
            pushed += 1
    for send in sends:
        send.wait_send()
    while pushed < 8:
        push(pushed)
        pushed += 1
    own = pltpu.make_async_copy(source.at[127], landed.at[127], own_sem)
    own.start()
    own.wait()

    def drained(ref, send, recv):
        return pltpu.make_async_remote_copy(
            src_ref=ref, dst_ref=ref, send_sem=send, recv_sem=recv,
            device_id=(me,), device_id_type=mesh_id,
        )

    blocks_in = drained(landed_blocks.at[pl.ds(0, count - 1)], block_send, block_recv)
    blocks_in.wait_recv()
    blocks_in.wait_send()
    landed_blocks[127:128, :] = block_rows[127:128, :]
    named = jnp.sum(landed_blocks[...].reshape(16, 8, 128), axis=1).astype(I32)

    def place(step, carry):
        base = pl.multiple_of(step * 256, 256)
        row = iota((256, 128), 0) + base
        for n in range(16):
            places[pl.ds(base, 256), 128 * n : 128 * n + 128] = onehot(row == named[n : n + 1, :])
        return carry

    lax.fori_loop(0, 8, place, 0)

    def unpack(chunk, chunks):
        for n in range(chunk, chunk + chunks):
            part = landed.at[pl.ds(16 * n, 15 if n == 7 else 16)]
            drained(part, send_sem, recv_sems.at[n]).wait_recv()
        values = landed[16 * chunk : 16 * chunk + 16 * chunks].reshape(256 * chunks, 128)
        upper = values.astype(BF)
        lower = (values - upper.astype(F32)).astype(BF)
        both = jnp.concatenate([upper, lower], axis=1)
        for part in range(4):
            at = slice(512 * part, 512 * part + 512)
            term = dot(places[at, 256 * chunk : 256 * chunk + 256 * chunks], both)
            term = term[:, 0:128] + term[:, 128:256]
            bricks[0, at, :] = term if chunk == 0 else bricks[0, at, :] + term

    for chunk, chunks in GROUPS:
        unpack(chunk, chunks)
    drained(source.at[pl.ds(0, count - 1)], send_sem, recv_sems.at[0]).wait_send()


def operators():
    d = diff_matrix()
    one = np.eye(8)
    op_x = np.kron(np.kron(d, one), one)
    op_y = np.kron(np.kron(np.eye(4), d), one)
    op_z = np.kron(np.eye(32), d)
    return [jnp.asarray(op, F32).astype(BF) for op in (op_x, np.concatenate([op_y, op_z]))]


def shards(velocity, inverse_sizes, resample_x, resample_y, resample_z, piece_target, target_brick, target_block, brick_home):
    op_x, op_yz = operators()
    ranks = np.zeros((8, 128), np.float32)
    for rank, (y, x, z, core) in enumerate(OFFSETS):
        ranks[:, ((y * 4 + x) * 4 + z) * 2 + core] = rank
    operands = (
        inverse_sizes, op_x, op_yz, jnp.asarray(ranks).astype(BF),
        piece_target, target_brick.reshape(1, 512), target_block.reshape(1, 512), brick_home.reshape(1, 128),
        resample_x, resample_y, resample_z, velocity,
    )
    scratch = [pltpu.VMEM(array.shape, array.dtype) for array in operands]
    scratch += [
        pltpu.VMEM((2, 9, 64, 128), F32),
        pltpu.VMEM((2, FACE, 128), F32),
        pltpu.VMEM((2, FACE, 128), F32),
        pltpu.VMEM((LAYERS, 9, 512, 128), F32),
        pltpu.VMEM((LAYERS, 512, 128), F32),
        pltpu.VMEM((512, 128), F32),
        pltpu.VMEM((128, 128), F32),
        pltpu.VMEM((1024, 256), BF),
        pltpu.VMEM((512, 1024), BF),
        pltpu.VMEM((1, 512), I32),
        pltpu.VMEM((512, 256), BF),
        pltpu.VMEM((128, 128), F32),
        pltpu.VMEM((128, SLOTS, 128), F32),
        pltpu.VMEM((128, SLOTS, 128), F32),
        pltpu.VMEM((128, 128), F32),
        pltpu.VMEM((BLOCKS, BLOCKS), BF),
        pltpu.SemaphoreType.DMA((len(operands) - 1,)),
        pltpu.SemaphoreType.DMA((3,)),
        pltpu.SemaphoreType.DMA((2,)),
        pltpu.SemaphoreType.DMA((2,)),
        pltpu.SemaphoreType.DMA,
        pltpu.SemaphoreType.DMA((8,)),
        pltpu.SemaphoreType.DMA,
        pltpu.SemaphoreType.DMA,
        pltpu.SemaphoreType.DMA,
    ]
    return pl.pallas_call(
        kernel,
        in_specs=[pl.BlockSpec(memory_space=pltpu.HBM)] * len(operands),
        out_specs=pl.BlockSpec(memory_space=pltpu.VMEM),
        out_shape=jax.ShapeDtypeStruct((1, BLOCKS, 128), F32),
        scratch_shapes=scratch,
        compiler_params=pltpu.CompilerParams(
            collective_id=0, has_side_effects=True, vmem_limit_bytes=VMEM_LIMIT
        ),
        name="step",
    )(*[pltpu.with_memory_space_constraint(operand, pltpu.HBM) for operand in operands])


def solution(mesh):
    return jax.shard_map(
        shards,
        mesh=mesh,
        in_specs=(
            P(None, None, "dom"),
            P(None, "dom"),
            P(None, None, None, "dom"),
            P(None, None, None, "dom"),
            P(None, None, None, "dom"),
            P(None, "dom"),
            P("dom", None),
            P("dom"),
            P(),
        ),
        out_specs=P("dom", None, None),
        check_vma=False,
    )
```
